32 devices in a mesh: win: 2 (over y), row: 4 (over z), col: 4 (over x, core).
Axes of the slice: x: 2, y: 2, z: 4, core: 2. Of those that a mesh axis runs over, the one named last changes fastest.
Arguments:
- mask_params: float32 [2048, 1024], P(('win', 'row'), 'col'), parts along dimension 0, may hold values from -4 to 4
- layout: int32 [8, 4, 4, 64], P(('win', 'row'), 'col'), parts along dimension 0, may hold values from 0 to 256, as said below
- kernels: float32 [2, 128, 12, 128], replicated, may hold values from -0.046875 to 0.046875
Outputs:
- updated: float32 [2048, 1024], P(('win', 'row'), 'col'), parts along dimension 0
The draws below stay inside these ranges and needn't reach their ends.
There are 2 independent parts, one for each index of `win`. The reference program is written for one: setup_inputs(seed, part) draws one part's arguments, and reference() takes and returns one part's arrays. A program takes and returns all parts, laid end to end along the dimension named above; an argument that names none is the same for every part. Nothing has to cross between parts.
Inputs may be any that keep to these rules, and one draw needn't show every extreme that they name: `layout`: in each tile every rectangle has first row < end row and first column < end column, in the tile's own pixel coordinates; rectangle 0 spans all 256 rows.
All inputs are finite; a program needn't handle non-finite values.
Results may differ from the reference program's by a relative error of at most 0.0082.
Values may be sent and summed in bfloat16 or wider, within the bound.
No kernel may reach another device: no remote copies, remote signals or barrier semaphores. Data moves between devices by JAX's collectives and lax.ppermute only.
A program may use at most 64 MiB of HBM per device.

```python
import math
import jax
import jax.numpy as jnp
from jax import lax

TILE = 256
MARGIN = 64
PERIOD = 384
FREQ = 128
KERNELS = 12
RECTS = 64
TILE_ROWS = 4
TILE_COLS = 4
NR = 1024
NC = 1024


def draw_layout(key, part):
    key_start = jax.random.fold_in(key, 11)
    key_span = jax.random.fold_in(key, 12)
    shape_all = (TILE_ROWS, TILE_COLS, 2, RECTS)
    starts = jax.random.randint(key_start, shape_all, 0, TILE)
    spans = jax.random.randint(key_span, shape_all, 1, TILE // 8 + 1)
    ends = jnp.minimum(starts + spans, TILE)
    first_rect = (jnp.arange(RECTS) == 0)[None, None, :]
    row_start = jnp.where(first_rect, 0, starts[:, :, 0])
    row_end = jnp.where(first_rect, TILE, ends[:, :, 0])
    return jnp.stack([row_start, row_end, starts[:, :, 1], ends[:, :, 1]], axis=2).astype(jnp.int32)


def levels(stream_key, shape, pieces, low, top_value):
    def one(axis_at, shards_of):
        heights = jax.random.uniform(jax.random.fold_in(jax.random.fold_in(stream_key, 6), axis_at), (shards_of,), jnp.float32, low / len(pieces), top_value / len(pieces))
        return jnp.repeat(jnp.exp(heights), shape[axis_at] // shards_of).reshape((-1,) + (1,) * (len(shape) - axis_at - 1))

    factor_of = one(*pieces[0])
    for cut in pieces[1:]:
        factor_of = factor_of * one(*cut)
    return factor_of


def bell_draw(key, dims, deviation, limit, shards=(), kind=jnp.bfloat16):
    factor_of = levels(key, dims, shards, -0.22, 0.18) if shards else 1.0
    entries = jax.random.normal(key, dims, jnp.float32) * deviation * factor_of
    return jnp.minimum(jnp.maximum(entries, -limit), limit).astype(kind)


def setup_inputs(seed: int = 0, part: int = 0) -> dict:
    keys = jax.random.split(jax.random.key(seed), 4)
    part_splits = jax.random.split(jax.random.fold_in(keys[3], part), 4)
    return {
        "mask_params": bell_draw(part_splits[0], (NR, NC), 1.0, 4.0, ((0, 4), (1, 4)), jnp.float32),
        "layout": draw_layout(jax.random.fold_in(jax.random.fold_in(keys[3], part), 71), part),
        "kernels": bell_draw(keys[2], (2, FREQ, KERNELS, FREQ), (1.0 / FREQ), 0.046875, (), jnp.float32),
    }


STEEPNESS = 2.0
CONTRAST = 4.0
THRESHOLD = 0.75
STEP_RATE = 1.0


def tables():
    frequency = jnp.arange(FREQ, dtype=jnp.int32) - FREQ // 2
    places = jnp.arange(PERIOD, dtype=jnp.int32)
    angles = jnp.mod(frequency[:, None] * places[None, :], PERIOD).astype(jnp.float32) * (2.0 * math.pi / PERIOD)
    return jnp.cos(angles).astype(jnp.bfloat16), jnp.sin(angles).astype(jnp.bfloat16)


def product(left_op, right_op):
    return jnp.dot(left_op, right_op, preferred_element_type=jnp.float32)


def raster(shapes):
    places = jnp.arange(TILE, dtype=jnp.int32)
    row_in = ((places[None, :] >= shapes[0][:, None]) & (places[None, :] < shapes[1][:, None])).astype(jnp.bfloat16)
    col_in = ((places[None, :] >= shapes[2][:, None]) & (places[None, :] < shapes[3][:, None])).astype(jnp.bfloat16)
    covered = product(row_in.T, col_in)
    return jnp.minimum(covered, 1.0)


def tile_gradient(extended, kernels, target, cos_t, sin_t):
    inner_cos = cos_t[:, MARGIN:MARGIN + TILE]
    inner_sin = sin_t[:, MARGIN:MARGIN + TILE]
    tables_both = jnp.concatenate([cos_t, sin_t], axis=0)
    spread = product(extended, tables_both.T)
    half_re = spread[:, :FREQ].astype(jnp.bfloat16)
    half_im = (-spread[:, FREQ:]).astype(jnp.bfloat16)
    spec_re = (product(cos_t, half_re) + product(sin_t, half_im)) / PERIOD
    spec_im = (product(cos_t, half_im) - product(sin_t, half_re)) / PERIOD
    kern_re = kernels[0]
    kern_im = kernels[1]
    mixed_re = (kern_re * spec_re[:, None, :] - kern_im * spec_im[:, None, :]).astype(jnp.bfloat16).reshape(FREQ * KERNELS, FREQ)
    mixed_im = (kern_re * spec_im[:, None, :] + kern_im * spec_re[:, None, :]).astype(jnp.bfloat16).reshape(FREQ * KERNELS, FREQ)
    line_re = (product(mixed_re, inner_cos) - product(mixed_im, inner_sin)).astype(jnp.bfloat16).reshape(FREQ, KERNELS * TILE)
    line_im = (product(mixed_re, inner_sin) + product(mixed_im, inner_cos)).astype(jnp.bfloat16).reshape(FREQ, KERNELS * TILE)
    field_re = product(inner_cos.T, line_re) - product(inner_sin.T, line_im)
    field_im = product(inner_cos.T, line_im) + product(inner_sin.T, line_re)
    field_re = field_re.reshape(TILE, KERNELS, TILE)
    field_im = field_im.reshape(TILE, KERNELS, TILE)
    intensity = jnp.sum(field_re * field_re + field_im * field_im, axis=1) / KERNELS
    resist = jax.nn.sigmoid(CONTRAST * (intensity - THRESHOLD))
    slope_err = 2.0 * (resist - target) * CONTRAST * resist * (1.0 - resist)
    weight = slope_err[:, None, :] * (2.0 / KERNELS)
    back_re = (field_re * weight).astype(jnp.bfloat16).reshape(TILE * KERNELS, TILE)
    back_im = (field_im * weight).astype(jnp.bfloat16).reshape(TILE * KERNELS, TILE)
    wave_re = (product(back_re, inner_cos.T) + product(back_im, inner_sin.T)).astype(jnp.bfloat16).reshape(TILE, KERNELS * FREQ)
    wave_im = (product(back_im, inner_cos.T) - product(back_re, inner_sin.T)).astype(jnp.bfloat16).reshape(TILE, KERNELS * FREQ)
    resp_re = (product(inner_cos, wave_re) + product(inner_sin, wave_im)).reshape(FREQ, KERNELS, FREQ)
    resp_im = (product(inner_cos, wave_im) - product(inner_sin, wave_re)).reshape(FREQ, KERNELS, FREQ)
    adj_re = (jnp.sum(kern_re * resp_re + kern_im * resp_im, axis=1) / PERIOD).astype(jnp.bfloat16)
    adj_im = (jnp.sum(kern_re * resp_im - kern_im * resp_re, axis=1) / PERIOD).astype(jnp.bfloat16)
    wide_re = (product(adj_re, cos_t) - product(adj_im, sin_t)).astype(jnp.bfloat16)
    wide_im = (product(adj_re, sin_t) + product(adj_im, cos_t)).astype(jnp.bfloat16)
    return product(cos_t.T, wide_re) - product(sin_t.T, wide_im)


def reference(mask_params, layout, kernels):
    cos_t, sin_t = tables()
    transmit = (2.0 * jax.nn.sigmoid(STEEPNESS * mask_params) - 1.0).astype(jnp.bfloat16)
    padded = jnp.pad(transmit, MARGIN)
    summed_all = jnp.zeros((NR + 2 * MARGIN, NC + 2 * MARGIN), jnp.float32)

    def visit_tile(tile_index, summed_all):
        row_tile = (tile_index // TILE_COLS).astype(jnp.int32)
        col_tile = (tile_index % TILE_COLS).astype(jnp.int32)
        row_at = (row_tile * TILE).astype(jnp.int32)
        col_at = (col_tile * TILE).astype(jnp.int32)
        extended = lax.dynamic_slice(padded, (row_at, col_at), (PERIOD, PERIOD))
        shapes = lax.dynamic_index_in_dim(lax.dynamic_index_in_dim(layout, row_tile, 0, False), col_tile, 0, False)
        target = raster(shapes)
        gradient = tile_gradient(extended, kernels, target, cos_t, sin_t)
        current = lax.dynamic_slice(summed_all, (row_at, col_at), (PERIOD, PERIOD))
        return lax.dynamic_update_slice(summed_all, current + gradient, (row_at, col_at))

    summed_all = lax.fori_loop(0, TILE_ROWS * TILE_COLS, visit_tile, summed_all)
    summed = summed_all[MARGIN:MARGIN + NR, MARGIN:MARGIN + NC]
    squashed = jax.nn.sigmoid(STEEPNESS * mask_params)
    return mask_params - STEP_RATE * summed * (2.0 * STEEPNESS) * squashed * (1.0 - squashed)
```

```python
import math

import jax
import jax.numpy as jnp
import ml_dtypes
import numpy as np
from jax import lax
from jax.experimental import pallas as pl
from jax.experimental.pallas import tpu as pltpu
from jax.sharding import PartitionSpec as P

TILE = 256
MARGIN = 64
PERIOD = 384
FREQ = 128
KERNELS = 12
STEEPNESS = 2.0
CONTRAST = 4.0
THRESHOLD = 0.75
STEP_RATE = 1.0

AXES = ("win", "row", "col")
MIB = 1 << 20


def table_constants():
    frequency = np.arange(FREQ, dtype=np.int64) - FREQ // 2
    places = np.arange(PERIOD, dtype=np.int64)
    angles = np.mod(frequency[:, None] * places[None, :], PERIOD) * (2.0 * math.pi / PERIOD)
    cos_t = np.cos(angles).astype(np.float32)
    sin_t = np.sin(angles).astype(np.float32)
    inner = slice(MARGIN, MARGIN + TILE)
    ci, si = cos_t[:, inner], sin_t[:, inner]
    names = dict(
        patch=np.concatenate([cos_t.T, -sin_t.T], axis=1),
        stack=np.concatenate([cos_t, sin_t], axis=0),
        inner=np.concatenate([ci, si], axis=0),
        fwd=np.block([[ci, si], [-si, ci]]),
        bwd=np.block([[ci.T, -si.T], [si.T, ci.T]]),
        wide=np.block([[cos_t, sin_t], [-sin_t, cos_t]]),
    )
    return {name: value.astype(ml_dtypes.bfloat16) for name, value in names.items()}


def dot(left, right):
    return jnp.dot(left, right, preferred_element_type=jnp.float32)


def call(kernel, outs, args, limit, name, scratch=(), flops=0, moved=0):
    return pl.pallas_call(
        kernel,
        out_shape=outs,
        in_specs=[pl.BlockSpec(memory_space=pltpu.VMEM)] * len(args),
        out_specs=jax.tree.map(lambda _: pl.BlockSpec(memory_space=pltpu.VMEM), outs),
        scratch_shapes=list(scratch),
        compiler_params=pltpu.CompilerParams(vmem_limit_bytes=limit),
        cost_estimate=pl.CostEstimate(flops=flops, bytes_accessed=moved, transcendentals=0),
        name=name,
    )(*args)


def is_even(axis):
    return lax.rem(lax.axis_index(axis), 2) == 0


def pick(even, first, second):
    return jnp.where(even, first, second)


def edges_kernel(mask_ref, transmit_ref, to_a_ref, to_b_ref):
    transmit = (2.0 * jax.nn.sigmoid(STEEPNESS * mask_ref[...]) - 1.0).astype(jnp.bfloat16)
    transmit_ref[...] = transmit
    top, bottom = transmit[:MARGIN], transmit[TILE - MARGIN :]
    even = is_even("row")
    to_a_ref[...] = pick(even, bottom, top)
    to_b_ref[...] = pick(even, top, bottom)


def strips_kernel(transmit_ref, from_a_ref, from_b_ref, middle_ref, to_a_ref, to_b_ref):
    row, rows = lax.axis_index("row"), lax.axis_size("row")
    even = is_even("row")
    a, b = from_a_ref[...], from_b_ref[...]
    zero = jnp.zeros_like(a)
    above = jnp.where(row == 0, zero, pick(even, b, a))
    below = jnp.where(row == rows - 1, zero, pick(even, a, b))
    middle_ref[:MARGIN] = above
    middle_ref[MARGIN : MARGIN + TILE] = transmit_ref[...]
    middle_ref[MARGIN + TILE :] = below
    left, right = pack(middle_ref, PERIOD // 2)
    even = is_even("col")
    to_a_ref[...] = pick(even, right, left)
    to_b_ref[...] = pick(even, left, right)


def pack(ref, half):
    width = ref.shape[1]
    first, last = ref[:, :128], ref[:, width - 128 :]
    left = jnp.concatenate([first[:half, :64], first[half:, :64]], axis=1)
    right = jnp.concatenate([last[half:, 64:], last[:half, 64:]], axis=1)
    return left, right


def received_columns(from_a_ref, from_b_ref):
    col, cols = lax.axis_index("col"), lax.axis_size("col")
    even = is_even("col")
    a, b = from_a_ref[...], from_b_ref[...]
    zero = jnp.zeros_like(a)
    from_right = jnp.where(col == cols - 1, zero, pick(even, a, b))
    from_left = jnp.where(col == 0, zero, pick(even, b, a))
    return from_right, from_left


def tile_kernel(
    middle_ref, from_a_ref, from_b_ref, kern_ref, rect_ref,
    patch_ref, stack_ref, inner_ref, fwd_ref, bwd_ref, wide_ref,
    to_a_ref, to_b_ref, grad_ref,
    field_ref, bright_ref, weight_ref, line_ref, adj_ref,
):
    half_rows = PERIOD // 2
    from_right, from_left = received_columns(from_a_ref, from_b_ref)
    low = lax.broadcasted_iota(jnp.int32, (half_rows, 128), 1) < 64
    upper = jnp.where(low, from_right, from_left)
    lower = jnp.where(low, from_left, from_right)
    head, tail = patch_ref[:MARGIN], patch_ref[MARGIN + TILE :]
    spread = dot(middle_ref[...], patch_ref[MARGIN : MARGIN + TILE])
    side_upper = dot(upper, jnp.concatenate([tail, head], axis=0))
    side_lower = dot(lower, jnp.concatenate([head, tail], axis=0))
    spread = spread + jnp.concatenate([side_upper, side_lower], axis=0)
    both = dot(stack_ref[...], spread.astype(jnp.bfloat16))
    spec_re = (both[:FREQ, :FREQ] + both[FREQ:, FREQ:]) / PERIOD
    spec_im = (both[:FREQ, FREQ:] - both[FREQ:, :FREQ]) / PERIOD

    for k in range(KERNELS):
        kern_re, kern_im = kern_ref[0, k], kern_ref[1, k]
        mixed_re = (kern_re * spec_re - kern_im * spec_im).astype(jnp.bfloat16)
        mixed_im = (kern_re * spec_im + kern_im * spec_re).astype(jnp.bfloat16)
        line = dot(jnp.concatenate([mixed_re, mixed_im], axis=1), fwd_ref[...])
        line = line.astype(jnp.bfloat16)
        line = jnp.concatenate([line[:, :TILE], line[:, TILE:]], axis=0)
        field = dot(bwd_ref[...], line)
        field_ref[k] = field
        field_re, field_im = field[:TILE], field[TILE:]
        power = field_re * field_re + field_im * field_im
        bright_ref[...] = power if k == 0 else bright_ref[...] + power

    places = lax.broadcasted_iota(jnp.int32, (TILE, 64), 0)
    rects = rect_ref[...]
    row_in = ((places >= rects[0:1]) & (places < rects[1:2])).astype(jnp.bfloat16)
    col_in = ((places >= rects[2:3]) & (places < rects[3:4])).astype(jnp.bfloat16)
    covered = lax.dot_general(
        row_in, col_in, (((1,), (1,)), ((), ())), preferred_element_type=jnp.float32
    )
    target = jnp.minimum(covered, 1.0)
    resist = jax.nn.sigmoid(CONTRAST * (bright_ref[...] / KERNELS - THRESHOLD))
    slope_err = 2.0 * (resist - target) * CONTRAST * resist * (1.0 - resist)
    weight_ref[...] = slope_err * (2.0 / KERNELS)

    for k in range(KERNELS):
        weight = weight_ref[...]
        back_re = (field_ref[k, :TILE] * weight).astype(jnp.bfloat16)
        back_im = (field_ref[k, TILE:] * weight).astype(jnp.bfloat16)
        wave = dot(jnp.concatenate([back_re, back_im], axis=1), bwd_ref[...])
        resp = dot(inner_ref[...], wave.astype(jnp.bfloat16))
        resp_re = resp[:FREQ, :FREQ] + resp[FREQ:, FREQ:]
        resp_im = resp[:FREQ, FREQ:] - resp[FREQ:, :FREQ]
        kern_re, kern_im = kern_ref[0, k], kern_ref[1, k]
        part_re = kern_re * resp_re + kern_im * resp_im
        part_im = kern_re * resp_im - kern_im * resp_re
        adj_ref[0] = part_re if k == 0 else adj_ref[0] + part_re
        adj_ref[1] = part_im if k == 0 else adj_ref[1] + part_im

    adj = jnp.concatenate([adj_ref[0] / PERIOD, adj_ref[1] / PERIOD], axis=1).astype(jnp.bfloat16)
    wide = dot(adj, wide_ref[...]).astype(jnp.bfloat16)
    gradient = dot(patch_ref[...], jnp.concatenate([wide[:, :PERIOD], wide[:, PERIOD:]], axis=0))
    top = gradient[:MARGIN].astype(jnp.bfloat16)
    bottom = gradient[MARGIN + TILE :].astype(jnp.bfloat16)
    even = is_even("row")
    to_a_ref[...] = pick(even, bottom, top)
    to_b_ref[...] = pick(even, top, bottom)
    grad_ref[...] = gradient[MARGIN : MARGIN + TILE]


def fold_kernel(grad_ref, from_a_ref, from_b_ref, core_ref, to_a_ref, to_b_ref, full_ref):
    row, rows = lax.axis_index("row"), lax.axis_size("row")
    even = is_even("row")
    a, b = from_a_ref[...].astype(jnp.float32), from_b_ref[...].astype(jnp.float32)
    zero = jnp.zeros_like(a)
    full_ref[...] = grad_ref[...]
    full_ref[:MARGIN] += jnp.where(row == 0, zero, pick(even, b, a))
    full_ref[TILE - MARGIN :] += jnp.where(row == rows - 1, zero, pick(even, a, b))
    left, right = pack(full_ref, TILE // 2)
    left, right = left.astype(jnp.bfloat16), right.astype(jnp.bfloat16)
    even = is_even("col")
    to_a_ref[...] = pick(even, right, left)
    to_b_ref[...] = pick(even, left, right)
    core_ref[...] = full_ref[:, MARGIN : MARGIN + TILE]


def update_kernel(mask_ref, core_ref, from_a_ref, from_b_ref, out_ref):
    half = TILE // 2
    from_right, from_left = received_columns(from_a_ref, from_b_ref)
    from_right = from_right.astype(jnp.float32)
    from_left = from_left.astype(jnp.float32)
    low = lax.broadcasted_iota(jnp.int32, (half, 128), 1) < 64
    zero = jnp.zeros((half, 128), jnp.float32)
    rolled_right = pltpu.roll(from_right, 64, 1)
    rolled_left = pltpu.roll(from_left, 64, 1)
    adds = (
        (jnp.where(low, rolled_left, zero), jnp.where(low, zero, rolled_right)),
        (jnp.where(low, from_left, zero), jnp.where(low, zero, from_right)),
    )
    for i, (first, last) in enumerate(adds):
        rows = slice(i * half, (i + 1) * half)
        for j, extra in enumerate((first, last)):
            cols = slice(j * 128, (j + 1) * 128)
            mask = mask_ref[rows, cols]
            squashed = jax.nn.sigmoid(STEEPNESS * mask)
            summed = core_ref[rows, cols] + extra
            out_ref[rows, cols] = mask - STEP_RATE * summed * (2.0 * STEEPNESS) * squashed * (
                1.0 - squashed
            )


def pairings(mesh):
    wins, rows, cols = (mesh.shape[axis] for axis in AXES)

    def flat(win, row, col):
        return (win * rows + row) * cols + col

    def row_b(win, row):
        other = row + 1 if row % 2 else row - 1
        if 0 <= other < rows:
            return win, other
        return (win ^ 1, row) if wins % 2 == 0 else (win, other % rows)

    partners = dict(
        row_a=lambda w, r, c: (w, r ^ 1, c),
        row_b=lambda w, r, c: (*row_b(w, r), c),
        col_a=lambda w, r, c: (w, r, c ^ 1),
        col_b=lambda w, r, c: (w, r, (c + 1 if c % 2 else c - 1) % cols),
    )
    places = [(w, r, c) for w in range(wins) for r in range(rows) for c in range(cols)]
    return {
        name: [(flat(*place), flat(*partner(*place))) for place in places]
        for name, partner in partners.items()
    }


def solution(mesh):
    assert mesh.shape["row"] % 2 == 0 and mesh.shape["col"] % 2 == 0
    pairs = pairings(mesh)
    tables = table_constants()

    def swap(axis, to_a, to_b):
        return (
            lax.ppermute(to_a, AXES, pairs[axis + "_a"]),
            lax.ppermute(to_b, AXES, pairs[axis + "_b"]),
        )

    def local(mask_params, layout, kernels):
        bf16, f32 = jnp.bfloat16, jnp.float32

        def shape(rows, cols, kind):
            return jax.ShapeDtypeStruct((rows, cols), kind)

        kernels = jnp.transpose(kernels, (0, 2, 1, 3))
        edge, strip = shape(MARGIN, TILE, bf16), shape(PERIOD // 2, 128, bf16)
        transmit, to_a, to_b = call(
            edges_kernel, (shape(TILE, TILE, bf16), edge, edge), (mask_params,), 2 * MIB, "edges"
        )
        middle, to_a, to_b = call(
            strips_kernel,
            (shape(PERIOD, TILE, bf16), strip, strip),
            (transmit, *swap("row", to_a, to_b)),
            2 * MIB,
            "strips",
        )
        edge = shape(MARGIN, PERIOD, bf16)
        to_a, to_b, grad = call(
            tile_kernel,
            (edge, edge, shape(TILE, PERIOD, f32)),
            (
                middle,
                *swap("col", to_a, to_b),
                kernels,
                layout[0, 0],
                *(jnp.asarray(tables[n]) for n in ("patch", "stack", "inner", "fwd", "bwd", "wide")),
            ),
            32 * MIB,
            "tile",
            scratch=(
                pltpu.VMEM((KERNELS, 2 * TILE, TILE), f32),
                pltpu.VMEM((TILE, TILE), f32),
                pltpu.VMEM((TILE, TILE), f32),
                pltpu.VMEM((TILE, TILE), bf16),
                pltpu.VMEM((2, FREQ, FREQ), f32),
            ),
            flops=2_700_000_000,
            moved=8_000_000,
        )
        strip = shape(TILE // 2, 128, bf16)
        core, to_a, to_b = call(
            fold_kernel,
            (shape(TILE, TILE, f32), strip, strip),
            (grad, *swap("row", to_a, to_b)),
            4 * MIB,
            "fold",
            scratch=(pltpu.VMEM((TILE, PERIOD), f32),),
        )
        return call(
            update_kernel,
            shape(TILE, TILE, f32),
            (mask_params, core, *swap("col", to_a, to_b)),
            4 * MIB,
            "update",
        )

    in_specs = (P(("win", "row"), "col"), P(("win", "row"), "col", None, None), P())
    out_specs = P(("win", "row"), "col")
    return jax.shard_map(local, mesh=mesh, in_specs=in_specs, out_specs=out_specs, check_vma=False)
```

```python
import math

import jax
import jax.numpy as jnp
import ml_dtypes
import numpy as np
from jax import lax
from jax.experimental import pallas as pl
from jax.experimental.pallas import tpu as pltpu
from jax.sharding import PartitionSpec as P

TILE = 256
MARGIN = 64
PERIOD = 384
FREQ = 128
KERNELS = 12
STEEPNESS = 2.0
CONTRAST = 4.0
THRESHOLD = 0.75
STEP_RATE = 1.0

AXES = ("win", "row", "col")
MIB = 1 << 20


def table_constants():
    frequency = np.arange(FREQ, dtype=np.int64) - FREQ // 2
    places = np.arange(PERIOD, dtype=np.int64)
    angles = np.mod(frequency[:, None] * places[None, :], PERIOD) * (2.0 * math.pi / PERIOD)
    cos_t = np.cos(angles).astype(np.float32)
    sin_t = np.sin(angles).astype(np.float32)
    inner = slice(MARGIN, MARGIN + TILE)
    ci, si = cos_t[:, inner], sin_t[:, inner]
    names = dict(
        patch=np.concatenate([cos_t.T, -sin_t.T], axis=1),
        stack=np.concatenate([cos_t, sin_t], axis=0),
        inner=np.concatenate([ci, si], axis=0),
        fwd=np.block([[ci, si], [-si, ci]]),
        bwd=np.block([[ci.T, -si.T], [si.T, ci.T]]),
        wide=np.block([[cos_t, sin_t], [-sin_t, cos_t]]),
    )
    return {name: value.astype(ml_dtypes.bfloat16) for name, value in names.items()}


def dot(left, right):
    return jnp.dot(left, right, preferred_element_type=jnp.float32)


def call(kernel, outs, args, limit, name, scratch=(), flops=0, moved=0):
    return pl.pallas_call(
        kernel,
        out_shape=outs,
        in_specs=[pl.BlockSpec(memory_space=pltpu.VMEM)] * len(args),
        out_specs=jax.tree.map(lambda _: pl.BlockSpec(memory_space=pltpu.VMEM), outs),
        scratch_shapes=list(scratch),
        compiler_params=pltpu.CompilerParams(vmem_limit_bytes=limit),
        cost_estimate=pl.CostEstimate(flops=flops, bytes_accessed=moved, transcendentals=0),
        name=name,
    )(*args)


def is_even(axis):
    return lax.rem(lax.axis_index(axis), 2) == 0


def pick(even, first, second):
    return jnp.where(even, first, second)


def edges_kernel(mask_ref, transmit_ref, to_a_ref, to_b_ref):
    transmit = (2.0 * jax.nn.sigmoid(STEEPNESS * mask_ref[...]) - 1.0).astype(jnp.bfloat16)
    transmit_ref[...] = transmit
    top, bottom = transmit[:MARGIN], transmit[TILE - MARGIN :]
    even = is_even("row")
    to_a_ref[...] = pick(even, bottom, top)
    to_b_ref[...] = pick(even, top, bottom)


def strips_kernel(transmit_ref, from_a_ref, from_b_ref, middle_ref, to_a_ref, to_b_ref):
    row, rows = lax.axis_index("row"), lax.axis_size("row")
    even = is_even("row")
    a, b = from_a_ref[...], from_b_ref[...]
    zero = jnp.zeros_like(a)
    above = jnp.where(row == 0, zero, pick(even, b, a))
    below = jnp.where(row == rows - 1, zero, pick(even, a, b))
    middle_ref[:MARGIN] = above
    middle_ref[MARGIN : MARGIN + TILE] = transmit_ref[...]
    middle_ref[MARGIN + TILE :] = below
    left, right = pack(middle_ref, PERIOD // 2)
    even = is_even("col")
    to_a_ref[...] = pick(even, right, left)
    to_b_ref[...] = pick(even, left, right)


def pack(ref, half):
    width = ref.shape[1]
    first, last = ref[:, :128], ref[:, width - 128 :]
    left = jnp.concatenate([first[:half, :64], first[half:, :64]], axis=1)
    right = jnp.concatenate([last[half:, 64:], last[:half, 64:]], axis=1)
    return left, right


def received_columns(from_a_ref, from_b_ref):
    col, cols = lax.axis_index("col"), lax.axis_size("col")
    even = is_even("col")
    a, b = from_a_ref[...], from_b_ref[...]
    zero = jnp.zeros_like(a)
    from_right = jnp.where(col == cols - 1, zero, pick(even, a, b))
    from_left = jnp.where(col == 0, zero, pick(even, b, a))
    return from_right, from_left


def prepare_kernel(rect_ref, *refs):
    count = (len(refs) - 2) // 2
    sources, target_ref, held, sems = refs[:count], refs[count], refs[count + 1 : -1], refs[-1]
    copies = [
        pltpu.make_async_copy(source, dest, sems.at[i])
        for i, (source, dest) in enumerate(zip(sources, held))
    ]
    for copy in copies:
        copy.start()
    rects = rect_ref[...]
    places = lax.broadcasted_iota(jnp.int32, (TILE, rects.shape[1]), 0)
    row_in = ((places >= rects[0:1]) & (places < rects[1:2])).astype(jnp.bfloat16)
    col_in = ((places >= rects[2:3]) & (places < rects[3:4])).astype(jnp.bfloat16)
    covered = lax.dot_general(
        row_in, col_in, (((1,), (1,)), ((), ())), preferred_element_type=jnp.float32
    )
    target_ref[...] = jnp.minimum(covered, 1.0)
    for copy in copies:
        copy.wait()


def prepare(rects, arrays):
    outs = (jax.ShapeDtypeStruct((TILE, TILE), jnp.float32),)
    outs += tuple(jax.ShapeDtypeStruct(array.shape, array.dtype) for array in arrays)
    return pl.pallas_call(
        prepare_kernel,
        out_shape=outs,
        in_specs=[pl.BlockSpec(memory_space=pltpu.VMEM)]
        + [pl.BlockSpec(memory_space=pltpu.HBM)] * len(arrays),
        out_specs=(pl.BlockSpec(memory_space=pltpu.VMEM),) * len(outs),
        scratch_shapes=[pltpu.SemaphoreType.DMA((len(arrays),))],
        compiler_params=pltpu.CompilerParams(vmem_limit_bytes=8 * MIB),
        cost_estimate=pl.CostEstimate(
            flops=1_000_000_000, bytes_accessed=3_000_000, transcendentals=0
        ),
        name="prepare",
    )(rects, *(pltpu.with_memory_space_constraint(array, pltpu.HBM) for array in arrays))


def pipeline(groups, first, second, third):
    def step(at, parity):
        static = isinstance(at, int)
        if not static or at >= 0:
            third(at, parity)
        if not static or -1 <= at < groups - 1:
            second(at + 1, 1 - parity)
        if not static or at < groups - 2:
            first(at + 2, parity)

    step(-2, 0)
    step(-1, 1)

    def body(i, carry):
        step(2 * i, 0)
        step(2 * i + 1, 1)
        return carry

    lax.fori_loop(0, (groups - 2) // 2, body, 0)
    step(groups - 2, 0)
    step(groups - 1, 1)


def tile_kernel(
    middle_ref, from_a_ref, from_b_ref, target_ref, kern_ref,
    patch_ref, stack_ref, inner_ref, fwd_ref, bwd_ref, wide_ref,
    to_a_ref, to_b_ref, grad_ref,
    field_ref, bright_ref, weight_ref, spec_ref, adj_ref, *slot_refs,
):
    mixed_refs, line_refs, back_refs, wave_refs = (slot_refs[i : i + 2] for i in (0, 2, 4, 6))
    half_rows = PERIOD // 2
    from_right, from_left = received_columns(from_a_ref, from_b_ref)
    low = lax.broadcasted_iota(jnp.int32, (half_rows, 128), 1) < 64
    upper = jnp.where(low, from_right, from_left)
    lower = jnp.where(low, from_left, from_right)
    head, tail = patch_ref[:MARGIN], patch_ref[MARGIN + TILE :]
    spread = dot(middle_ref[...], patch_ref[MARGIN : MARGIN + TILE])
    side_upper = dot(upper, jnp.concatenate([tail, head], axis=0))
    side_lower = dot(lower, jnp.concatenate([head, tail], axis=0))
    spread = spread + jnp.concatenate([side_upper, side_lower], axis=0)
    both = dot(stack_ref[...], spread.astype(jnp.bfloat16))
    spec_re = (both[:FREQ, :FREQ] + both[FREQ:, FREQ:]) / PERIOD
    spec_im = (both[:FREQ, FREQ:] - both[FREQ:, :FREQ]) / PERIOD

    spec_ref[0], spec_ref[1] = spec_re, spec_im
    groups = KERNELS // 2

    def mix(group, slot):
        for j in range(2):
            k = 2 * group + j
            kern_re, kern_im = kern_ref[0, k], kern_ref[1, k]
            spec_re, spec_im = spec_ref[0], spec_ref[1]
            rows = slice(j * FREQ, (j + 1) * FREQ)
            mixed_re = kern_re * spec_re - kern_im * spec_im
            mixed_im = kern_re * spec_im + kern_im * spec_re
            mixed_refs[slot][rows, :FREQ] = mixed_re.astype(jnp.bfloat16)
            mixed_refs[slot][rows, FREQ:] = mixed_im.astype(jnp.bfloat16)

    def expand(group, slot):
        line = dot(mixed_refs[slot][...], fwd_ref[...]).astype(jnp.bfloat16)
        for j in range(2):
            rows = slice(j * FREQ, (j + 1) * FREQ)
            line_refs[slot][j, :FREQ] = line[rows, :TILE]
            line_refs[slot][j, FREQ:] = line[rows, TILE:]

    def image(group, slot):
        total = bright_ref[...]
        for j in range(2):
            field = dot(bwd_ref[...], line_refs[slot][j])
            field_ref[2 * group + j] = field
            total = total + (field[:TILE] * field[:TILE] + field[TILE:] * field[TILE:])
        bright_ref[...] = total

    bright_ref[...] = jnp.zeros_like(bright_ref)
    pipeline(groups, mix, expand, image)

    resist = jax.nn.sigmoid(CONTRAST * (bright_ref[...] / KERNELS - THRESHOLD))
    slope_err = 2.0 * (resist - target_ref[...]) * CONTRAST * resist * (1.0 - resist)
    weight_ref[...] = slope_err * (2.0 / KERNELS)

    def weigh(group, slot):
        for j in range(2):
            rows = slice(j * TILE, (j + 1) * TILE)
            weight = weight_ref[...]
            back_re = field_ref[2 * group + j, :TILE] * weight
            back_im = field_ref[2 * group + j, TILE:] * weight
            back_refs[slot][rows, :TILE] = back_re.astype(jnp.bfloat16)
            back_refs[slot][rows, TILE:] = back_im.astype(jnp.bfloat16)

    def contract(group, slot):
        wave_refs[slot][...] = dot(back_refs[slot][...], bwd_ref[...]).astype(jnp.bfloat16)

    def respond(group, slot):
        adj_re, adj_im = adj_ref[0], adj_ref[1]
        for j in range(2):
            resp = dot(inner_ref[...], wave_refs[slot][j * TILE : (j + 1) * TILE])
            resp_re = resp[:FREQ, :FREQ] + resp[FREQ:, FREQ:]
            resp_im = resp[:FREQ, FREQ:] - resp[FREQ:, :FREQ]
            kern_re, kern_im = kern_ref[0, 2 * group + j], kern_ref[1, 2 * group + j]
            adj_re = adj_re + (kern_re * resp_re + kern_im * resp_im)
            adj_im = adj_im + (kern_re * resp_im - kern_im * resp_re)
        adj_ref[0], adj_ref[1] = adj_re, adj_im

    adj_ref[...] = jnp.zeros_like(adj_ref)
    pipeline(groups, weigh, contract, respond)

    adj = jnp.concatenate([adj_ref[0] / PERIOD, adj_ref[1] / PERIOD], axis=1).astype(jnp.bfloat16)
    wide = dot(adj, wide_ref[...]).astype(jnp.bfloat16)
    gradient = dot(patch_ref[...], jnp.concatenate([wide[:, :PERIOD], wide[:, PERIOD:]], axis=0))
    top = gradient[:MARGIN].astype(jnp.bfloat16)
    bottom = gradient[MARGIN + TILE :].astype(jnp.bfloat16)
    even = is_even("row")
    to_a_ref[...] = pick(even, bottom, top)
    to_b_ref[...] = pick(even, top, bottom)
    grad_ref[...] = gradient[MARGIN : MARGIN + TILE]


def fold_kernel(grad_ref, from_a_ref, from_b_ref, core_ref, to_a_ref, to_b_ref, full_ref):
    row, rows = lax.axis_index("row"), lax.axis_size("row")
    even = is_even("row")
    a, b = from_a_ref[...].astype(jnp.float32), from_b_ref[...].astype(jnp.float32)
    zero = jnp.zeros_like(a)
    full_ref[...] = grad_ref[...]
    full_ref[:MARGIN] += jnp.where(row == 0, zero, pick(even, b, a))
    full_ref[TILE - MARGIN :] += jnp.where(row == rows - 1, zero, pick(even, a, b))
    left, right = pack(full_ref, TILE // 2)
    left, right = left.astype(jnp.bfloat16), right.astype(jnp.bfloat16)
    even = is_even("col")
    to_a_ref[...] = pick(even, right, left)
    to_b_ref[...] = pick(even, left, right)
    core_ref[...] = full_ref[:, MARGIN : MARGIN + TILE]


def update_kernel(mask_ref, core_ref, from_a_ref, from_b_ref, out_ref):
    half = TILE // 2
    from_right, from_left = received_columns(from_a_ref, from_b_ref)
    from_right = from_right.astype(jnp.float32)
    from_left = from_left.astype(jnp.float32)
    low = lax.broadcasted_iota(jnp.int32, (half, 128), 1) < 64
    zero = jnp.zeros((half, 128), jnp.float32)
    rolled_right = pltpu.roll(from_right, 64, 1)
    rolled_left = pltpu.roll(from_left, 64, 1)
    adds = (
        (jnp.where(low, rolled_left, zero), jnp.where(low, zero, rolled_right)),
        (jnp.where(low, from_left, zero), jnp.where(low, zero, from_right)),
    )
    for i, (first, last) in enumerate(adds):
        rows = slice(i * half, (i + 1) * half)
        for j, extra in enumerate((first, last)):
            cols = slice(j * 128, (j + 1) * 128)
            mask = mask_ref[rows, cols]
            squashed = jax.nn.sigmoid(STEEPNESS * mask)
            summed = core_ref[rows, cols] + extra
            out_ref[rows, cols] = mask - STEP_RATE * summed * (2.0 * STEEPNESS) * squashed * (
                1.0 - squashed
            )


def pairings(mesh):
    wins, rows, cols = (mesh.shape[axis] for axis in AXES)

    def flat(win, row, col):
        return (win * rows + row) * cols + col

    def row_b(win, row):
        other = row + 1 if row % 2 else row - 1
        if 0 <= other < rows:
            return win, other
        return (win ^ 1, row) if wins % 2 == 0 else (win, other % rows)

    partners = dict(
        row_a=lambda w, r, c: (w, r ^ 1, c),
        row_b=lambda w, r, c: (*row_b(w, r), c),
        col_a=lambda w, r, c: (w, r, c ^ 1),
        col_b=lambda w, r, c: (w, r, (c + 1 if c % 2 else c - 1) % cols),
    )
    places = [(w, r, c) for w in range(wins) for r in range(rows) for c in range(cols)]
    return {
        name: [(flat(*place), flat(*partner(*place))) for place in places]
        for name, partner in partners.items()
    }


def solution(mesh):
    assert mesh.shape["row"] % 2 == 0 and mesh.shape["col"] % 2 == 0
    pairs = pairings(mesh)
    tables = table_constants()

    def swap(axis, to_a, to_b):
        return (
            lax.ppermute(to_a, AXES, pairs[axis + "_a"]),
            lax.ppermute(to_b, AXES, pairs[axis + "_b"]),
        )

    def local(mask_params, layout, kernels):
        bf16, f32 = jnp.bfloat16, jnp.float32

        def shape(rows, cols, kind):
            return jax.ShapeDtypeStruct((rows, cols), kind)

        kernels = jnp.transpose(kernels, (0, 2, 1, 3))
        edge, strip = shape(MARGIN, TILE, bf16), shape(PERIOD // 2, 128, bf16)
        transmit, to_a, to_b = call(
            edges_kernel, (shape(TILE, TILE, bf16), edge, edge), (mask_params,), 2 * MIB, "edges"
        )
        middle, to_a, to_b = call(
            strips_kernel,
            (shape(PERIOD, TILE, bf16), strip, strip),
            (transmit, *swap("row", to_a, to_b)),
            2 * MIB,
            "strips",
        )
        names = ("patch", "stack", "inner", "fwd", "bwd", "wide")
        held = prepare(layout[0, 0], [kernels, *(jnp.asarray(tables[name]) for name in names)])
        edge = shape(MARGIN, PERIOD, bf16)
        to_a, to_b, grad = call(
            tile_kernel,
            (edge, edge, shape(TILE, PERIOD, f32)),
            (
                middle,
                *swap("col", to_a, to_b),
                *held,
            ),
            32 * MIB,
            "tile",
            scratch=(
                pltpu.VMEM((KERNELS, 2 * TILE, TILE), f32),
                pltpu.VMEM((TILE, TILE), f32),
                pltpu.VMEM((TILE, TILE), f32),
                pltpu.VMEM((2, FREQ, FREQ), f32),
                pltpu.VMEM((2, FREQ, FREQ), f32),
                *[pltpu.VMEM((2 * FREQ, 2 * FREQ), bf16)] * 2,
                *[pltpu.VMEM((2, 2 * FREQ, TILE), bf16)] * 2,
                *[pltpu.VMEM((2 * TILE, 2 * TILE), bf16)] * 2,
                *[pltpu.VMEM((2 * TILE, 2 * FREQ), bf16)] * 2,
            ),
            flops=2_700_000_000,
            moved=8_000_000,
        )
        strip = shape(TILE // 2, 128, bf16)
        core, to_a, to_b = call(
            fold_kernel,
            (shape(TILE, TILE, f32), strip, strip),
            (grad, *swap("row", to_a, to_b)),
            4 * MIB,
            "fold",
            scratch=(pltpu.VMEM((TILE, PERIOD), f32),),
        )
        return call(
            update_kernel,
            shape(TILE, TILE, f32),
            (mask_params, core, *swap("col", to_a, to_b)),
            4 * MIB,
            "update",
        )

    in_specs = (P(("win", "row"), "col"), P(("win", "row"), "col", None, None), P())
    out_specs = P(("win", "row"), "col")
    return jax.shard_map(local, mesh=mesh, in_specs=in_specs, out_specs=out_specs, check_vma=False)
```

```python
import math

import jax
import jax.numpy as jnp
import ml_dtypes
import numpy as np
from jax import lax
from jax.experimental import pallas as pl
from jax.experimental.pallas import tpu as pltpu
from jax.sharding import PartitionSpec as P

TILE = 256
MARGIN = 64
PERIOD = 384
FREQ = 128
KERNELS = 12
STEEPNESS = 2.0
CONTRAST = 4.0
THRESHOLD = 0.75
STEP_RATE = 1.0

AXES = ("win", "row", "col")
MIB = 1 << 20


def table_constants():
    frequency = np.arange(FREQ, dtype=np.int64) - FREQ // 2
    places = np.arange(PERIOD, dtype=np.int64)
    angles = np.mod(frequency[:, None] * places[None, :], PERIOD) * (2.0 * math.pi / PERIOD)
    cos_t = np.cos(angles).astype(np.float32)
    sin_t = np.sin(angles).astype(np.float32)
    inner = slice(MARGIN, MARGIN + TILE)
    ci, si = cos_t[:, inner], sin_t[:, inner]
    names = dict(
        patch=np.concatenate([cos_t.T, -sin_t.T], axis=1),
        stack=np.concatenate([cos_t, sin_t], axis=0),
        inner=np.concatenate([ci, si], axis=0),
        fwd=np.block([[ci, si], [-si, ci]]),
        bwd=np.block([[ci.T, -si.T], [si.T, ci.T]]),
        wide=np.block([[cos_t, sin_t], [-sin_t, cos_t]]),
    )
    return {name: value.astype(ml_dtypes.bfloat16) for name, value in names.items()}


def dot(left, right):
    return jnp.dot(left, right, preferred_element_type=jnp.float32)


def call(kernel, outs, args, limit, name, scratch=(), flops=0, moved=0):
    return pl.pallas_call(
        kernel,
        out_shape=outs,
        in_specs=[pl.BlockSpec(memory_space=pltpu.VMEM)] * len(args),
        out_specs=jax.tree.map(lambda _: pl.BlockSpec(memory_space=pltpu.VMEM), outs),
        scratch_shapes=list(scratch),
        compiler_params=pltpu.CompilerParams(vmem_limit_bytes=limit),
        cost_estimate=pl.CostEstimate(flops=flops, bytes_accessed=moved, transcendentals=0),
        name=name,
    )(*args)


def is_even(axis):
    return lax.rem(lax.axis_index(axis), 2) == 0


def pick(even, first, second):
    return jnp.where(even, first, second)


def edges_kernel(mask_ref, transmit_ref, to_a_ref, to_b_ref):
    transmit = (2.0 * jax.nn.sigmoid(STEEPNESS * mask_ref[...]) - 1.0).astype(jnp.bfloat16)
    transmit_ref[...] = transmit
    top, bottom = transmit[:MARGIN], transmit[TILE - MARGIN :]
    even = is_even("row")
    to_a_ref[...] = pick(even, bottom, top)
    to_b_ref[...] = pick(even, top, bottom)


def strips_kernel(transmit_ref, from_a_ref, from_b_ref, middle_ref, to_a_ref, to_b_ref):
    row, rows = lax.axis_index("row"), lax.axis_size("row")
    even = is_even("row")
    a, b = from_a_ref[...], from_b_ref[...]
    zero = jnp.zeros_like(a)
    above = jnp.where(row == 0, zero, pick(even, b, a))
    below = jnp.where(row == rows - 1, zero, pick(even, a, b))
    middle_ref[:MARGIN] = above
    middle_ref[MARGIN : MARGIN + TILE] = transmit_ref[...]
    middle_ref[MARGIN + TILE :] = below
    left, right = pack(middle_ref, PERIOD // 2)
    even = is_even("col")
    to_a_ref[...] = pick(even, right, left)
    to_b_ref[...] = pick(even, left, right)


def pack(ref, half):
    width = ref.shape[1]
    first, last = ref[:, :128], ref[:, width - 128 :]
    left = jnp.concatenate([first[:half, :64], first[half:, :64]], axis=1)
    right = jnp.concatenate([last[half:, 64:], last[:half, 64:]], axis=1)
    return left, right


def received_columns(from_a_ref, from_b_ref):
    col, cols = lax.axis_index("col"), lax.axis_size("col")
    even = is_even("col")
    a, b = from_a_ref[...], from_b_ref[...]
    zero = jnp.zeros_like(a)
    from_right = jnp.where(col == cols - 1, zero, pick(even, a, b))
    from_left = jnp.where(col == 0, zero, pick(even, b, a))
    return from_right, from_left


def prepare_kernel(rect_ref, *refs):
    count = (len(refs) - 2) // 2
    sources, target_ref, held, sems = refs[:count], refs[count], refs[count + 1 : -1], refs[-1]
    copies = [
        pltpu.make_async_copy(source, dest, sems.at[i])
        for i, (source, dest) in enumerate(zip(sources, held))
    ]
    for copy in copies:
        copy.start()
    rects = rect_ref[...]
    places = lax.broadcasted_iota(jnp.int32, (TILE, rects.shape[1]), 0)
    row_in = ((places >= rects[0:1]) & (places < rects[1:2])).astype(jnp.bfloat16)
    col_in = ((places >= rects[2:3]) & (places < rects[3:4])).astype(jnp.bfloat16)
    covered = lax.dot_general(
        row_in, col_in, (((1,), (1,)), ((), ())), preferred_element_type=jnp.float32
    )
    target_ref[...] = jnp.minimum(covered, 1.0)
    for copy in copies:
        copy.wait()


def prepare(rects, arrays):
    outs = (jax.ShapeDtypeStruct((TILE, TILE), jnp.float32),)
    outs += tuple(jax.ShapeDtypeStruct(array.shape, array.dtype) for array in arrays)
    return pl.pallas_call(
        prepare_kernel,
        out_shape=outs,
        in_specs=[pl.BlockSpec(memory_space=pltpu.VMEM)]
        + [pl.BlockSpec(memory_space=pltpu.HBM)] * len(arrays),
        out_specs=(pl.BlockSpec(memory_space=pltpu.VMEM),) * len(outs),
        scratch_shapes=[pltpu.SemaphoreType.DMA((len(arrays),))],
        compiler_params=pltpu.CompilerParams(vmem_limit_bytes=8 * MIB),
        cost_estimate=pl.CostEstimate(
            flops=1_000_000_000, bytes_accessed=3_000_000, transcendentals=0
        ),
        name="prepare",
    )(rects, *(pltpu.with_memory_space_constraint(array, pltpu.HBM) for array in arrays))


def pipeline(groups, first, second, third):
    def step(at, parity):
        static = isinstance(at, int)
        if not static or -1 <= at < groups - 1:
            second(at + 1, 1 - parity)
        if not static or at >= 0:
            third(at, parity)
        if not static or at < groups - 2:
            first(at + 2, parity)

    for at in range(-2, groups):
        step(at, at % 2)


def tile_kernel(
    middle_ref, from_a_ref, from_b_ref, target_ref, kern_ref,
    patch_ref, stack_ref, inner_ref, fwd_ref, bwd_ref, wide_ref,
    to_a_ref, to_b_ref, grad_ref,
    field_ref, bright_ref, weight_ref, spec_ref, adj_ref, *slot_refs,
):
    mixed_refs, line_refs, back_refs, wave_refs = (slot_refs[i : i + 2] for i in (0, 2, 4, 6))
    half_rows = PERIOD // 2
    from_right, from_left = received_columns(from_a_ref, from_b_ref)
    low = lax.broadcasted_iota(jnp.int32, (half_rows, 128), 1) < 64
    upper = jnp.where(low, from_right, from_left)
    lower = jnp.where(low, from_left, from_right)
    head, tail = patch_ref[:MARGIN], patch_ref[MARGIN + TILE :]
    spread = dot(middle_ref[...], patch_ref[MARGIN : MARGIN + TILE])
    side_upper = dot(upper, jnp.concatenate([tail, head], axis=0))
    side_lower = dot(lower, jnp.concatenate([head, tail], axis=0))
    spread = spread + jnp.concatenate([side_upper, side_lower], axis=0)
    both = dot(stack_ref[...], spread.astype(jnp.bfloat16))
    spec_re = (both[:FREQ, :FREQ] + both[FREQ:, FREQ:]) / PERIOD
    spec_im = (both[:FREQ, FREQ:] - both[FREQ:, :FREQ]) / PERIOD

    spec_ref[0], spec_ref[1] = spec_re, spec_im
    groups = KERNELS // 2

    def mix(group, slot):
        for j in range(2):
            k = 2 * group + j
            kern_re, kern_im = kern_ref[0, k], kern_ref[1, k]
            spec_re, spec_im = spec_ref[0], spec_ref[1]
            rows = slice(j * FREQ, (j + 1) * FREQ)
            mixed_re = kern_re * spec_re - kern_im * spec_im
            mixed_im = kern_re * spec_im + kern_im * spec_re
            mixed_refs[slot][rows, :FREQ] = mixed_re.astype(jnp.bfloat16)
            mixed_refs[slot][rows, FREQ:] = mixed_im.astype(jnp.bfloat16)

    def expand(group, slot):
        line = dot(mixed_refs[slot][...], fwd_ref[...]).astype(jnp.bfloat16)
        for j in range(2):
            rows = slice(j * FREQ, (j + 1) * FREQ)
            line_refs[slot][j, :FREQ] = line[rows, :TILE]
            line_refs[slot][j, FREQ:] = line[rows, TILE:]

    def image(group, slot):
        total = bright_ref[...]
        for j in range(2):
            field = dot(bwd_ref[...], line_refs[slot][j])
            field_ref[2 * group + j] = field
            total = total + (field[:TILE] * field[:TILE] + field[TILE:] * field[TILE:])
        bright_ref[...] = total

    bright_ref[...] = jnp.zeros_like(bright_ref)
    pipeline(groups, mix, expand, image)

    half_turn = jnp.tanh(
        bright_ref[...] * (CONTRAST / (2.0 * KERNELS)) - CONTRAST * THRESHOLD / 2.0
    )
    slope = (2.0 * CONTRAST / 4.0) * (2.0 / KERNELS) * (1.0 - half_turn * half_turn)
    weight_ref[...] = (0.5 + 0.5 * half_turn - target_ref[...]) * slope

    def weigh(group, slot):
        for j in range(2):
            rows = slice(j * TILE, (j + 1) * TILE)
            weight = weight_ref[...]
            back_re = field_ref[2 * group + j, :TILE] * weight
            back_im = field_ref[2 * group + j, TILE:] * weight
            back_refs[slot][rows, :TILE] = back_re.astype(jnp.bfloat16)
            back_refs[slot][rows, TILE:] = back_im.astype(jnp.bfloat16)

    def contract(group, slot):
        for j in range(2):
            rows = slice(j * TILE, (j + 1) * TILE)
            wave = dot(back_refs[slot][rows], bwd_ref[...])
            wave_refs[slot][rows] = wave.astype(jnp.bfloat16)

    def respond(group, slot):
        adj_re, adj_im = adj_ref[0], adj_ref[1]
        for j in range(2):
            resp = dot(inner_ref[...], wave_refs[slot][j * TILE : (j + 1) * TILE])
            resp_re = resp[:FREQ, :FREQ] + resp[FREQ:, FREQ:]
            resp_im = resp[:FREQ, FREQ:] - resp[FREQ:, :FREQ]
            kern_re, kern_im = kern_ref[0, 2 * group + j], kern_ref[1, 2 * group + j]
            adj_re = adj_re + (kern_re * resp_re + kern_im * resp_im)
            adj_im = adj_im + (kern_re * resp_im - kern_im * resp_re)
        adj_ref[0], adj_ref[1] = adj_re, adj_im

    adj_ref[...] = jnp.zeros_like(adj_ref)
    pipeline(groups, weigh, contract, respond)

    adj = jnp.concatenate([adj_ref[0] / PERIOD, adj_ref[1] / PERIOD], axis=1).astype(jnp.bfloat16)
    wide = dot(adj, wide_ref[...]).astype(jnp.bfloat16)
    gradient = dot(patch_ref[...], jnp.concatenate([wide[:, :PERIOD], wide[:, PERIOD:]], axis=0))
    top = gradient[:MARGIN].astype(jnp.bfloat16)
    bottom = gradient[MARGIN + TILE :].astype(jnp.bfloat16)
    even = is_even("row")
    to_a_ref[...] = pick(even, bottom, top)
    to_b_ref[...] = pick(even, top, bottom)
    grad_ref[...] = gradient[MARGIN : MARGIN + TILE]


def fold_kernel(grad_ref, from_a_ref, from_b_ref, core_ref, to_a_ref, to_b_ref, full_ref):
    row, rows = lax.axis_index("row"), lax.axis_size("row")
    even = is_even("row")
    a, b = from_a_ref[...].astype(jnp.float32), from_b_ref[...].astype(jnp.float32)
    zero = jnp.zeros_like(a)
    full_ref[...] = grad_ref[...]
    full_ref[:MARGIN] += jnp.where(row == 0, zero, pick(even, b, a))
    full_ref[TILE - MARGIN :] += jnp.where(row == rows - 1, zero, pick(even, a, b))
    left, right = pack(full_ref, TILE // 2)
    left, right = left.astype(jnp.bfloat16), right.astype(jnp.bfloat16)
    even = is_even("col")
    to_a_ref[...] = pick(even, right, left)
    to_b_ref[...] = pick(even, left, right)
    core_ref[...] = full_ref[:, MARGIN : MARGIN + TILE]


def update_kernel(mask_ref, core_ref, from_a_ref, from_b_ref, out_ref):
    half = TILE // 2
    from_right, from_left = received_columns(from_a_ref, from_b_ref)
    from_right = from_right.astype(jnp.float32)
    from_left = from_left.astype(jnp.float32)
    low = lax.broadcasted_iota(jnp.int32, (half, 128), 1) < 64
    zero = jnp.zeros((half, 128), jnp.float32)
    rolled_right = pltpu.roll(from_right, 64, 1)
    rolled_left = pltpu.roll(from_left, 64, 1)
    adds = (
        (jnp.where(low, rolled_left, zero), jnp.where(low, zero, rolled_right)),
        (jnp.where(low, from_left, zero), jnp.where(low, zero, from_right)),
    )
    for i, (first, last) in enumerate(adds):
        rows = slice(i * half, (i + 1) * half)
        for j, extra in enumerate((first, last)):
            cols = slice(j * 128, (j + 1) * 128)
            mask = mask_ref[rows, cols]
            squashed = jax.nn.sigmoid(STEEPNESS * mask)
            summed = core_ref[rows, cols] + extra
            out_ref[rows, cols] = mask - STEP_RATE * summed * (2.0 * STEEPNESS) * squashed * (
                1.0 - squashed
            )


def pairings(mesh):
    wins, rows, cols = (mesh.shape[axis] for axis in AXES)

    def flat(win, row, col):
        return (win * rows + row) * cols + col

    def row_b(win, row):
        other = row + 1 if row % 2 else row - 1
        if 0 <= other < rows:
            return win, other
        return (win ^ 1, row) if wins % 2 == 0 else (win, other % rows)

    partners = dict(
        row_a=lambda w, r, c: (w, r ^ 1, c),
        row_b=lambda w, r, c: (*row_b(w, r), c),
        col_a=lambda w, r, c: (w, r, c ^ 1),
        col_b=lambda w, r, c: (w, r, (c + 1 if c % 2 else c - 1) % cols),
    )
    places = [(w, r, c) for w in range(wins) for r in range(rows) for c in range(cols)]
    return {
        name: [(flat(*place), flat(*partner(*place))) for place in places]
        for name, partner in partners.items()
    }


def solution(mesh):
    assert mesh.shape["row"] % 2 == 0 and mesh.shape["col"] % 2 == 0
    pairs = pairings(mesh)
    tables = table_constants()

    def swap(axis, to_a, to_b):
        return (
            lax.ppermute(to_a, AXES, pairs[axis + "_a"]),
            lax.ppermute(to_b, AXES, pairs[axis + "_b"]),
        )

    def local(mask_params, layout, kernels):
        bf16, f32 = jnp.bfloat16, jnp.float32

        def shape(rows, cols, kind):
            return jax.ShapeDtypeStruct((rows, cols), kind)

        kernels = jnp.transpose(kernels, (0, 2, 1, 3))
        edge, strip = shape(MARGIN, TILE, bf16), shape(PERIOD // 2, 128, bf16)
        transmit, to_a, to_b = call(
            edges_kernel, (shape(TILE, TILE, bf16), edge, edge), (mask_params,), 2 * MIB, "edges"
        )
        middle, to_a, to_b = call(
            strips_kernel,
            (shape(PERIOD, TILE, bf16), strip, strip),
            (transmit, *swap("row", to_a, to_b)),
            2 * MIB,
            "strips",
        )
        names = ("patch", "stack", "inner", "fwd", "bwd", "wide")
        held = prepare(layout[0, 0], [kernels, *(jnp.asarray(tables[name]) for name in names)])
        edge = shape(MARGIN, PERIOD, bf16)
        to_a, to_b, grad = call(
            tile_kernel,
            (edge, edge, shape(TILE, PERIOD, f32)),
            (
                middle,
                *swap("col", to_a, to_b),
                *held,
            ),
            32 * MIB,
            "tile",
            scratch=(
                pltpu.VMEM((KERNELS, 2 * TILE, TILE), f32),
                pltpu.VMEM((TILE, TILE), f32),
                pltpu.VMEM((TILE, TILE), f32),
                pltpu.VMEM((2, FREQ, FREQ), f32),
                pltpu.VMEM((2, FREQ, FREQ), f32),
                *[pltpu.VMEM((2 * FREQ, 2 * FREQ), bf16)] * 2,
                *[pltpu.VMEM((2, 2 * FREQ, TILE), bf16)] * 2,
                *[pltpu.VMEM((2 * TILE, 2 * TILE), bf16)] * 2,
                *[pltpu.VMEM((2 * TILE, 2 * FREQ), bf16)] * 2,
            ),
            flops=2_700_000_000,
            moved=8_000_000,
        )
        strip = shape(TILE // 2, 128, bf16)
        core, to_a, to_b = call(
            fold_kernel,
            (shape(TILE, TILE, f32), strip, strip),
            (grad, *swap("row", to_a, to_b)),
            4 * MIB,
            "fold",
            scratch=(pltpu.VMEM((TILE, PERIOD), f32),),
        )
        return call(
            update_kernel,
            shape(TILE, TILE, f32),
            (mask_params, core, *swap("col", to_a, to_b)),
            4 * MIB,
            "update",
        )

    in_specs = (P(("win", "row"), "col"), P(("win", "row"), "col", None, None), P())
    out_specs = P(("win", "row"), "col")
    return jax.shard_map(local, mesh=mesh, in_specs=in_specs, out_specs=out_specs, check_vma=False)
```

```python
import functools
import math

import jax
import jax.numpy as jnp
import ml_dtypes
import numpy as np
from jax import lax
from jax.experimental import pallas as pl
from jax.experimental.pallas import tpu as pltpu
from jax.sharding import PartitionSpec as P

TILE = 256
MARGIN = 64
PERIOD = 384
FREQ = 128
KERNELS = 12
STEEPNESS = 2.0
CONTRAST = 4.0
THRESHOLD = 0.75
STEP_RATE = 1.0

AXES = ("win", "row", "col")
MIB = 1 << 20


def table_constants():
    frequency = np.arange(FREQ, dtype=np.int64) - FREQ // 2
    places = np.arange(PERIOD, dtype=np.int64)
    angles = np.mod(frequency[:, None] * places[None, :], PERIOD) * (2.0 * math.pi / PERIOD)
    cos_t = np.cos(angles).astype(np.float32)
    sin_t = np.sin(angles).astype(np.float32)
    inner = np.arange(MARGIN, MARGIN + TILE)
    rim = np.concatenate([np.arange(MARGIN), np.arange(MARGIN + TILE, PERIOD)])
    ci, si, cm, sm = cos_t[:, inner], sin_t[:, inner], cos_t[:, rim], sin_t[:, rim]
    names = dict(
        inner=np.concatenate([ci, si], axis=0),
        rim=np.concatenate([cm, sm], axis=0),
        patch=np.concatenate([cos_t.T, -sin_t.T], axis=1),
        fwd=np.block([[ci, si], [-si, ci]]),
        bwd=np.block([[ci.T, -si.T], [si.T, ci.T]]),
        margin=np.block([[cm, sm], [-sm, cm]]),
    )
    return {name: value.astype(ml_dtypes.bfloat16) for name, value in names.items()}


def dot(left, right):
    return jnp.dot(left, right, preferred_element_type=jnp.float32)


VMEM = pl.BlockSpec(memory_space=pltpu.VMEM)
HBM = pl.BlockSpec(memory_space=pltpu.HBM)


def call(kernel, outs, args, limit, name, scratch=(), flops=0, moved=0, hbm=(), hbm_out=(), **more):
    args = [
        pltpu.with_memory_space_constraint(arg, pltpu.HBM) if i in hbm else arg
        for i, arg in enumerate(args)
    ]
    return pl.pallas_call(
        kernel,
        out_shape=outs,
        in_specs=[HBM if i in hbm else VMEM for i in range(len(args))],
        out_specs=tuple(HBM if i in hbm_out else VMEM for i in range(len(outs))),
        scratch_shapes=list(scratch),
        compiler_params=pltpu.CompilerParams(vmem_limit_bytes=limit),
        cost_estimate=pl.CostEstimate(flops=flops, bytes_accessed=moved, transcendentals=0),
        name=name,
        **more,
    )(*args)


def is_even(axis):
    return lax.rem(lax.axis_index(axis), 2) == 0


def route(axis, back, ahead, to_a_ref, to_b_ref):
    even = is_even(axis)
    to_a_ref[...] = jnp.where(even, ahead, back)
    to_b_ref[...] = jnp.where(even, back, ahead)


def arrived(axis, from_a_ref, from_b_ref):
    even, at, size = is_even(axis), lax.axis_index(axis), lax.axis_size(axis)
    a, b = from_a_ref[...], from_b_ref[...]
    zero = jnp.zeros_like(a)
    before = jnp.where(at == 0, zero, jnp.where(even, b, a))
    after = jnp.where(at == size - 1, zero, jnp.where(even, a, b))
    return before, after


def low_lanes(rows):
    return lax.broadcasted_iota(jnp.int32, (rows, 128), 1) < 64


def pack(first, second):
    low, turned = low_lanes(FREQ), pltpu.roll(second, 64, 1)
    return jnp.where(low, first, turned), jnp.where(low, turned, first)


def to_transmit(mask):
    return (2.0 * jax.nn.sigmoid(STEEPNESS * mask) - 1.0).astype(jnp.bfloat16)


def edges_kernel(mask_ref, to_a_ref, to_b_ref, rows_ref, sems):
    copies = [
        pltpu.make_async_copy(mask_ref.at[pl.ds(start, MARGIN)], rows_ref.at[i], sems.at[i])
        for i, start in enumerate((0, TILE - MARGIN))
    ]
    for copy in copies:
        copy.start()
    for copy in copies:
        copy.wait()
    route("row", to_transmit(rows_ref[0]), to_transmit(rows_ref[1]), to_a_ref, to_b_ref)


def prepare_kernel(count, mask_ref, rect_ref, *refs):
    sources, target_ref, rows_ref, held = refs[:count], refs[count], refs[count + 1], refs[count + 2 : 2 * count + 2]
    mask_buf, rect_buf, sems = refs[2 * count + 2 :]
    moves = [(rect_ref, rect_buf), (mask_ref, mask_buf), *zip(sources, held)]
    copies = [
        pltpu.make_async_copy(source, dest, sems.at[i]) for i, (source, dest) in enumerate(moves)
    ]
    for copy in copies:
        copy.start()
    copies[0].wait()
    rects = rect_buf[...]
    places = lax.broadcasted_iota(jnp.int32, (TILE, rects.shape[1]), 0)
    row_in = ((places >= rects[0:1]) & (places < rects[1:2])).astype(jnp.bfloat16)
    col_in = ((places >= rects[2:3]) & (places < rects[3:4])).astype(jnp.bfloat16)
    covered = lax.dot_general(
        row_in, col_in, (((1,), (1,)), ((), ())), preferred_element_type=jnp.float32
    )
    target_ref[...] = jnp.minimum(covered, 1.0)
    copies[1].wait()
    transmit = to_transmit(mask_buf[...])
    copies[2].wait()
    rows_ref[...] = dot(held[0][...], transmit)
    for copy in copies[3:]:
        copy.wait()


def strips_kernel(rows_ref, from_a_ref, from_b_ref, rim_ref, out_ref, to_a_ref, to_b_ref):
    above, below = arrived("row", from_a_ref, from_b_ref)
    halo = jnp.concatenate([above, below], axis=0)
    parts = []
    for half in (slice(0, FREQ), slice(FREQ, 2 * FREQ)):
        part = (rows_ref[half] + dot(rim_ref[half], halo)).astype(jnp.bfloat16)
        out_ref[half] = part
        parts.append(part)
    low = low_lanes(FREQ)
    first, second = (jnp.where(low, part[:, :128], part[:, 128:]) for part in parts)
    left, right = pack(first, second)
    route("col", left, right, to_a_ref, to_b_ref)


def inside_kernel(rows_ref, patch_ref, out_ref):
    for half in (slice(0, FREQ), slice(FREQ, 2 * FREQ)):
        out_ref[half] = dot(rows_ref[half], patch_ref[MARGIN : MARGIN + TILE])


def pipeline(groups, first, second, third):
    def step(at, parity):
        static = isinstance(at, int)
        if not static or -1 <= at < groups - 1:
            second(at + 1, 1 - parity)
        if not static or at >= 0:
            third(at, parity)
        if not static or at < groups - 2:
            first(at + 2, parity)

    for at in range(-2, groups):
        step(at, at % 2)


def tile_kernel(
    inside_ref, from_a_ref, from_b_ref, target_ref, kern_ref,
    inner_ref, rim_ref, patch_ref, fwd_ref, bwd_ref, margin_ref,
    to_a_ref, to_b_ref, wide_ref,
    field_ref, bright_ref, weight_ref, spec_ref, adj_ref, *slot_refs,
):
    del rim_ref
    mixed_refs, line_refs, back_refs, wave_refs = (slot_refs[i : i + 2] for i in (0, 2, 4, 6))
    from_left, from_right = arrived("col", from_a_ref, from_b_ref)
    low = low_lanes(FREQ)
    head, tail = patch_ref[:MARGIN], patch_ref[MARGIN + TILE :]
    first = dot(jnp.where(low, from_right, from_left), jnp.concatenate([tail, head], axis=0))
    second = dot(jnp.where(low, from_left, from_right), jnp.concatenate([head, tail], axis=0))
    first, second = first + inside_ref[:FREQ], second + inside_ref[FREQ:]
    spec_re = (first[:, :FREQ] + second[:, FREQ:]) / PERIOD
    spec_im = (first[:, FREQ:] - second[:, :FREQ]) / PERIOD
    spec_ref[0], spec_ref[1] = spec_re, spec_im
    groups = KERNELS // 2

    def mix(group, slot):
        for j in range(2):
            k = 2 * group + j
            kern_re, kern_im = kern_ref[0, k], kern_ref[1, k]
            spec_re, spec_im = spec_ref[0], spec_ref[1]
            rows = slice(j * FREQ, (j + 1) * FREQ)
            mixed_re = kern_re * spec_re - kern_im * spec_im
            mixed_im = kern_re * spec_im + kern_im * spec_re
            mixed_refs[slot][rows, :FREQ] = mixed_re.astype(jnp.bfloat16)
            mixed_refs[slot][rows, FREQ:] = mixed_im.astype(jnp.bfloat16)

    def expand(group, slot):
        line = dot(mixed_refs[slot][...], fwd_ref[...]).astype(jnp.bfloat16)
        for j in range(2):
            rows = slice(j * FREQ, (j + 1) * FREQ)
            line_refs[slot][j, :FREQ] = line[rows, :TILE]
            line_refs[slot][j, FREQ:] = line[rows, TILE:]

    def image(group, slot):
        total = bright_ref[...]
        for j in range(2):
            field = dot(bwd_ref[...], line_refs[slot][j])
            field_ref[2 * group + j] = field
            total = total + (field[:TILE] * field[:TILE] + field[TILE:] * field[TILE:])
        bright_ref[...] = total

    bright_ref[...] = jnp.zeros_like(bright_ref)
    pipeline(groups, mix, expand, image)

    half_turn = jnp.tanh(
        bright_ref[...] * (CONTRAST / (2.0 * KERNELS)) - CONTRAST * THRESHOLD / 2.0
    )
    slope = (2.0 * CONTRAST / 4.0) * (2.0 / KERNELS) * (1.0 - half_turn * half_turn)
    weight_ref[...] = (0.5 + 0.5 * half_turn - target_ref[...]) * slope

    def weigh(group, slot):
        for j in range(2):
            rows = slice(j * TILE, (j + 1) * TILE)
            weight = weight_ref[...]
            back_re = field_ref[2 * group + j, :TILE] * weight
            back_im = field_ref[2 * group + j, TILE:] * weight
            back_refs[slot][rows, :TILE] = back_re.astype(jnp.bfloat16)
            back_refs[slot][rows, TILE:] = back_im.astype(jnp.bfloat16)

    def contract(group, slot):
        for j in range(2):
            rows = slice(j * TILE, (j + 1) * TILE)
            wave = dot(back_refs[slot][rows], bwd_ref[...])
            wave_refs[slot][rows] = wave.astype(jnp.bfloat16)

    def respond(group, slot):
        adj_re, adj_im = adj_ref[0], adj_ref[1]
        for j in range(2):
            resp = dot(inner_ref[...], wave_refs[slot][j * TILE : (j + 1) * TILE])
            resp_re = resp[:FREQ, :FREQ] + resp[FREQ:, FREQ:]
            resp_im = resp[:FREQ, FREQ:] - resp[FREQ:, :FREQ]
            kern_re, kern_im = kern_ref[0, 2 * group + j], kern_ref[1, 2 * group + j]
            adj_re = adj_re + (kern_re * resp_re + kern_im * resp_im)
            adj_im = adj_im + (kern_re * resp_im - kern_im * resp_re)
        adj_ref[0], adj_ref[1] = adj_re, adj_im

    adj_ref[...] = jnp.zeros_like(adj_ref)
    pipeline(groups, weigh, contract, respond)

    adj = jnp.concatenate([adj_ref[0] / PERIOD, adj_ref[1] / PERIOD], axis=1).astype(jnp.bfloat16)
    margin = dot(adj, margin_ref[...])
    left, right = pack(margin[:, :FREQ], margin[:, FREQ:])
    route("col", left.astype(jnp.bfloat16), right.astype(jnp.bfloat16), to_a_ref, to_b_ref)
    wide = dot(adj, fwd_ref[...])
    wide_ref[:FREQ] = wide[:, :TILE]
    wide_ref[FREQ:] = wide[:, TILE:]


def fold_kernel(wide_ref, from_a_ref, from_b_ref, patch_ref, out_ref, to_a_ref, to_b_ref):
    from_left, from_right = arrived("col", from_a_ref, from_b_ref)
    from_left, from_right = from_left.astype(jnp.float32), from_right.astype(jnp.float32)
    low, zero = low_lanes(FREQ), jnp.zeros((FREQ, 128), jnp.float32)
    turned_left, turned_right = pltpu.roll(from_left, 64, 1), pltpu.roll(from_right, 64, 1)
    first_half, second_half = slice(0, FREQ), slice(FREQ, 2 * FREQ)
    for half, left, right in (
        (first_half, turned_left, turned_right),
        (second_half, from_left, from_right),
    ):
        added = wide_ref[half, :128] + jnp.where(low, left, zero)
        out_ref[half, :128] = added.astype(jnp.bfloat16)
        added = wide_ref[half, 128:] + jnp.where(low, zero, right)
        out_ref[half, 128:] = added.astype(jnp.bfloat16)
    wide = out_ref[...]
    top = dot(patch_ref[:MARGIN], wide).astype(jnp.bfloat16)
    bottom = dot(patch_ref[MARGIN + TILE :], wide).astype(jnp.bfloat16)
    route("row", top, bottom, to_a_ref, to_b_ref)


def core_kernel(wide_ref, patch_ref, mask_ref, out_ref, rim_ref, rate_ref, rows_ref, sem):
    wide = wide_ref[...]
    ends = (slice(0, MARGIN), slice(MARGIN, TILE - MARGIN), slice(TILE - MARGIN, TILE))
    for i, rows in enumerate(ends):
        shifted = slice(rows.start + MARGIN, rows.stop + MARGIN)
        mask = mask_ref[rows]
        squashed = jax.nn.sigmoid(STEEPNESS * mask)
        rate = STEP_RATE * (2.0 * STEEPNESS) * squashed * (1.0 - squashed)
        updated = mask - dot(patch_ref[shifted], wide) * rate
        if i == 1:
            rows_ref[...] = updated
        else:
            rim_ref[i // 2], rate_ref[i // 2] = updated, rate
    copy = pltpu.make_async_copy(rows_ref, out_ref.at[pl.ds(MARGIN, TILE - 2 * MARGIN)], sem)
    copy.start()
    copy.wait()


def finish_kernel(most_ref, rim_ref, rate_ref, from_a_ref, from_b_ref, out_ref, rows_ref, sems):
    del most_ref
    copies = []
    for i, strip in enumerate(arrived("row", from_a_ref, from_b_ref)):
        rows_ref[i] = rim_ref[i] - strip.astype(jnp.float32) * rate_ref[i]
        start = i * (TILE - MARGIN)
        copy = pltpu.make_async_copy(rows_ref.at[i], out_ref.at[pl.ds(start, MARGIN)], sems.at[i])
        copy.start()
        copies.append(copy)
    for copy in copies:
        copy.wait()


def pairings(mesh):
    wins, rows, cols = (mesh.shape[axis] for axis in AXES)

    def flat(win, row, col):
        return (win * rows + row) * cols + col

    def row_b(win, row):
        other = row + 1 if row % 2 else row - 1
        if 0 <= other < rows:
            return win, other
        return (win ^ 1, row) if wins % 2 == 0 else (win, other % rows)

    partners = dict(
        row_a=lambda w, r, c: (w, r ^ 1, c),
        row_b=lambda w, r, c: (*row_b(w, r), c),
        col_a=lambda w, r, c: (w, r, c ^ 1),
        col_b=lambda w, r, c: (w, r, (c + 1 if c % 2 else c - 1) % cols),
    )
    places = [(w, r, c) for w in range(wins) for r in range(rows) for c in range(cols)]
    return {
        name: [(flat(*place), flat(*partner(*place))) for place in places]
        for name, partner in partners.items()
    }


def solution(mesh):
    assert mesh.shape["row"] % 2 == 0 and mesh.shape["col"] % 2 == 0
    pairs = pairings(mesh)
    tables = table_constants()
    bf16, f32 = jnp.bfloat16, jnp.float32
    shape = jax.ShapeDtypeStruct
    edge, strip = shape((MARGIN, TILE), bf16), shape((FREQ, 128), bf16)
    whole = shape((TILE, TILE), f32)
    dma = pltpu.SemaphoreType.DMA

    def swap(axis, to_a, to_b):
        return (
            lax.ppermute(to_a, AXES, pairs[axis + "_a"]),
            lax.ppermute(to_b, AXES, pairs[axis + "_b"]),
        )

    def local(mask_params, layout, kernels):
        edges = call(
            edges_kernel, (edge, edge), (mask_params,), 2 * MIB, "edges", hbm=(0,),
            scratch=(pltpu.VMEM((2, MARGIN, TILE), f32), dma((2,))),
        )
        inner, *others = (jnp.asarray(table) for table in tables.values())
        arrays = [inner, *others, jnp.transpose(kernels, (0, 2, 1, 3))]
        target, rows, *held, kern = call(
            functools.partial(prepare_kernel, len(arrays)),
            (whole, whole, *(shape(array.shape, array.dtype) for array in arrays)),
            (mask_params, layout[0, 0], *arrays),
            8 * MIB,
            "prepare",
            hbm=range(len(arrays) + 2),
            scratch=(
                pltpu.VMEM((TILE, TILE), f32),
                pltpu.VMEM(layout.shape[2:], jnp.int32),
                dma((len(arrays) + 2,)),
            ),
            flops=1_000_000_000,
            moved=3_000_000,
        )
        held = dict(zip(tables, held))
        rows, *strips = call(
            strips_kernel,
            (shape((2 * FREQ, TILE), bf16), strip, strip),
            (rows, *swap("row", *edges), held["rim"]),
            2 * MIB,
            "strips",
        )
        (inside,) = call(
            inside_kernel, (whole,), (rows, held["patch"]), 2 * MIB, "inside",
            flops=100_000_000, moved=600_000,
        )
        *strips, wide = call(
            tile_kernel,
            (strip, strip, whole),
            (inside, *swap("col", *strips), target, kern, *held.values()),
            32 * MIB,
            "tile",
            scratch=(
                pltpu.VMEM((KERNELS, 2 * TILE, TILE), f32),
                pltpu.VMEM((TILE, TILE), f32),
                pltpu.VMEM((TILE, TILE), f32),
                pltpu.VMEM((2, FREQ, FREQ), f32),
                pltpu.VMEM((2, FREQ, FREQ), f32),
                *[pltpu.VMEM((2 * FREQ, 2 * FREQ), bf16)] * 2,
                *[pltpu.VMEM((2, 2 * FREQ, TILE), bf16)] * 2,
                *[pltpu.VMEM((2 * TILE, 2 * TILE), bf16)] * 2,
                *[pltpu.VMEM((2 * TILE, 2 * FREQ), bf16)] * 2,
            ),
            flops=2_500_000_000,
            moved=8_000_000,
        )
        wide, *edges = call(
            fold_kernel,
            (shape((2 * FREQ, TILE), bf16), edge, edge),
            (wide, *swap("col", *strips), held["patch"]),
            4 * MIB,
            "fold",
        )
        ends = shape((2, MARGIN, TILE), f32)
        most, rim, rate = call(
            core_kernel,
            (whole, ends, ends),
            (wide, held["patch"], mask_params),
            4 * MIB,
            "core",
            hbm_out=(0,),
            scratch=(pltpu.VMEM((TILE - 2 * MARGIN, TILE), f32), dma(())),
            flops=200_000_000,
            moved=1_000_000,
        )
        (updated,) = call(
            finish_kernel,
            (whole,),
            (most, rim, rate, *swap("row", *edges)),
            4 * MIB,
            "finish",
            hbm=(0,),
            hbm_out=(0,),
            scratch=(pltpu.VMEM((2, MARGIN, TILE), f32), dma((2,))),
            input_output_aliases={0: 0},
        )
        return updated

    in_specs = (P(("win", "row"), "col"), P(("win", "row"), "col", None, None), P())
    out_specs = P(("win", "row"), "col")
    return jax.shard_map(local, mesh=mesh, in_specs=in_specs, out_specs=out_specs, check_vma=False)
```

```python
import functools
import math

import jax
import jax.numpy as jnp
import ml_dtypes
import numpy as np
from jax import lax
from jax.experimental import pallas as pl
from jax.experimental.pallas import tpu as pltpu
from jax.sharding import PartitionSpec as P

TILE = 256
MARGIN = 64
PERIOD = 384
FREQ = 128
KERNELS = 12
STEEPNESS = 2.0
CONTRAST = 4.0
THRESHOLD = 0.75
STEP_RATE = 1.0

AXES = ("win", "row", "col")
MIB = 1 << 20
PIECES = 1


def table_constants():
    frequency = np.arange(FREQ, dtype=np.int64) - FREQ // 2
    places = np.arange(PERIOD, dtype=np.int64)
    angles = np.mod(frequency[:, None] * places[None, :], PERIOD) * (2.0 * math.pi / PERIOD)
    cos_t = np.cos(angles).astype(np.float32)
    sin_t = np.sin(angles).astype(np.float32)
    inner = np.arange(MARGIN, MARGIN + TILE)
    rim = np.concatenate([np.arange(MARGIN), np.arange(MARGIN + TILE, PERIOD)])
    ci, si, cm, sm = cos_t[:, inner], sin_t[:, inner], cos_t[:, rim], sin_t[:, rim]
    names = dict(
        inner=np.concatenate([ci, si], axis=0),
        rim=np.concatenate([cm, sm], axis=0),
        patch=np.concatenate([cos_t.T, -sin_t.T], axis=1),
        fwd=np.block([[ci, si], [-si, ci]]),
        bwd=np.block([[ci.T, -si.T], [si.T, ci.T]]),
        margin=np.block([[cm, sm], [-sm, cm]]),
    )
    return {name: value.astype(ml_dtypes.bfloat16) for name, value in names.items()}


def dot(left, right):
    return jnp.dot(left, right, preferred_element_type=jnp.float32)


VMEM = pl.BlockSpec(memory_space=pltpu.VMEM)
HBM = pl.BlockSpec(memory_space=pltpu.HBM)


def call(kernel, outs, args, limit, name, scratch=(), flops=0, moved=0, hbm=(), hbm_out=(), flags=None, **more):
    args = [
        pltpu.with_memory_space_constraint(arg, pltpu.HBM) if i in hbm else arg
        for i, arg in enumerate(args)
    ]
    return pl.pallas_call(
        kernel,
        out_shape=outs,
        in_specs=[HBM if i in hbm else VMEM for i in range(len(args))],
        out_specs=tuple(HBM if i in hbm_out else VMEM for i in range(len(outs))),
        scratch_shapes=list(scratch),
        compiler_params=pltpu.CompilerParams(vmem_limit_bytes=limit, flags=flags),
        cost_estimate=pl.CostEstimate(flops=flops, bytes_accessed=moved, transcendentals=0),
        name=name,
        **more,
    )(*args)


def is_even(axis):
    return lax.rem(lax.axis_index(axis), 2) == 0


def route(axis, back, ahead, to_a_ref, to_b_ref):
    even = is_even(axis)
    to_a_ref[...] = jnp.where(even, ahead, back)
    to_b_ref[...] = jnp.where(even, back, ahead)


def arrived(axis, from_a_ref, from_b_ref):
    even, at, size = is_even(axis), lax.axis_index(axis), lax.axis_size(axis)
    a, b = from_a_ref[...], from_b_ref[...]
    zero = jnp.zeros_like(a)
    before = jnp.where(at == 0, zero, jnp.where(even, b, a))
    after = jnp.where(at == size - 1, zero, jnp.where(even, a, b))
    return before, after


def low_lanes(rows):
    return lax.broadcasted_iota(jnp.int32, (rows, 128), 1) < 64


def pack(first, second):
    low, turned = low_lanes(FREQ), pltpu.roll(second, 64, 1)
    return jnp.where(low, first, turned), jnp.where(low, turned, first)


def to_transmit(mask):
    return (2.0 * jax.nn.sigmoid(STEEPNESS * mask) - 1.0).astype(jnp.bfloat16)


def edges_kernel(mask_ref, to_a_ref, to_b_ref, rows_ref, sems):
    chunk = MARGIN // PIECES
    copies = [
        pltpu.make_async_copy(
            mask_ref.at[pl.ds(start + j * chunk, chunk)],
            rows_ref.at[i, pl.ds(j * chunk, chunk)],
            sems.at[i * PIECES + j],
        )
        for i, start in enumerate((0, TILE - MARGIN))
        for j in range(PIECES)
    ]
    for copy in copies:
        copy.start()
    for copy in copies:
        copy.wait()
    route("row", to_transmit(rows_ref[0]), to_transmit(rows_ref[1]), to_a_ref, to_b_ref)


def prepare_kernel(count, mask_ref, rect_ref, *refs):
    sources, target_ref, rows_ref, held = refs[:count], refs[count], refs[count + 1], refs[count + 2 : 2 * count + 2]
    mask_buf, rect_buf, sems = refs[2 * count + 2 :]
    moves = [(rect_ref, rect_buf), (mask_ref, mask_buf), *zip(sources, held)]
    copies = [
        pltpu.make_async_copy(source, dest, sems.at[i]) for i, (source, dest) in enumerate(moves)
    ]
    for copy in copies:
        copy.start()
    copies[0].wait()
    rects = rect_buf[...]
    places = lax.broadcasted_iota(jnp.int32, (TILE, rects.shape[1]), 0)
    row_in = ((places >= rects[0:1]) & (places < rects[1:2])).astype(jnp.bfloat16)
    col_in = ((places >= rects[2:3]) & (places < rects[3:4])).astype(jnp.bfloat16)
    covered = lax.dot_general(
        row_in, col_in, (((1,), (1,)), ((), ())), preferred_element_type=jnp.float32
    )
    target_ref[...] = jnp.minimum(covered, 1.0)
    copies[1].wait()
    transmit = to_transmit(mask_buf[...])
    copies[2].wait()
    rows_ref[...] = dot(held[0][...], transmit)
    for copy in copies[3:]:
        copy.wait()


def strips_kernel(rows_ref, from_a_ref, from_b_ref, rim_ref, out_ref, to_a_ref, to_b_ref):
    above, below = arrived("row", from_a_ref, from_b_ref)
    halo = jnp.concatenate([above, below], axis=0)
    parts = []
    for half in (slice(0, FREQ), slice(FREQ, 2 * FREQ)):
        part = (rows_ref[half] + dot(rim_ref[half], halo)).astype(jnp.bfloat16)
        out_ref[half] = part
        parts.append(part)
    low = low_lanes(FREQ)
    first, second = (jnp.where(low, part[:, :128], part[:, 128:]) for part in parts)
    left, right = pack(first, second)
    route("col", left, right, to_a_ref, to_b_ref)


def inside_kernel(rows_ref, patch_ref, out_ref):
    for half in (slice(0, FREQ), slice(FREQ, 2 * FREQ)):
        out_ref[half] = dot(rows_ref[half], patch_ref[MARGIN : MARGIN + TILE])


def pipeline(groups, first, second, third):
    def step(at, parity):
        static = isinstance(at, int)
        if not static or -1 <= at < groups - 1:
            second(at + 1, 1 - parity)
        if not static or at >= 0:
            third(at, parity)
        if not static or at < groups - 2:
            first(at + 2, parity)

    for at in range(-2, groups):
        step(at, at % 2)


def tile_kernel(
    inside_ref, from_a_ref, from_b_ref, target_ref, kern_ref,
    inner_ref, rim_ref, patch_ref, fwd_ref, bwd_ref, margin_ref,
    to_a_ref, to_b_ref, out_ref,
    field_ref, bright_ref, weight_ref, spec_ref, adj_ref, *slot_refs,
):
    del rim_ref
    mixed_refs, line_refs, back_refs, wave_refs = (slot_refs[i : i + 2] for i in (0, 2, 4, 6))
    from_left, from_right = arrived("col", from_a_ref, from_b_ref)
    low = low_lanes(FREQ)
    head, tail = patch_ref[:MARGIN], patch_ref[MARGIN + TILE :]
    first = dot(jnp.where(low, from_right, from_left), jnp.concatenate([tail, head], axis=0))
    second = dot(jnp.where(low, from_left, from_right), jnp.concatenate([head, tail], axis=0))
    first, second = first + inside_ref[:FREQ], second + inside_ref[FREQ:]
    spec_re = (first[:, :FREQ] + second[:, FREQ:]) / PERIOD
    spec_im = (first[:, FREQ:] - second[:, :FREQ]) / PERIOD
    spec_ref[0], spec_ref[1] = spec_re, spec_im
    groups = KERNELS // 2

    def mix(group, slot):
        for j in range(2):
            k = 2 * group + j
            kern_re, kern_im = kern_ref[0, k], kern_ref[1, k]
            spec_re, spec_im = spec_ref[0], spec_ref[1]
            rows = slice(j * FREQ, (j + 1) * FREQ)
            mixed_re = kern_re * spec_re - kern_im * spec_im
            mixed_im = kern_re * spec_im + kern_im * spec_re
            mixed_refs[slot][rows, :FREQ] = mixed_re.astype(jnp.bfloat16)
            mixed_refs[slot][rows, FREQ:] = mixed_im.astype(jnp.bfloat16)

    def expand(group, slot):
        line = dot(mixed_refs[slot][...], fwd_ref[...]).astype(jnp.bfloat16)
        for j in range(2):
            rows = slice(j * FREQ, (j + 1) * FREQ)
            line_refs[slot][j, :FREQ] = line[rows, :TILE]
            line_refs[slot][j, FREQ:] = line[rows, TILE:]

    def image(group, slot):
        total = bright_ref[...]
        for j in range(2):
            field = dot(bwd_ref[...], line_refs[slot][j])
            field_ref[2 * group + j] = field
            total = total + (field[:TILE] * field[:TILE] + field[TILE:] * field[TILE:])
        bright_ref[...] = total

    bright_ref[...] = jnp.zeros_like(bright_ref)
    pipeline(groups, mix, expand, image)

    half_turn = jnp.tanh(
        bright_ref[...] * (CONTRAST / (2.0 * KERNELS)) - CONTRAST * THRESHOLD / 2.0
    )
    slope = (2.0 * CONTRAST / 4.0) * (2.0 / KERNELS) * (1.0 - half_turn * half_turn)
    weight_ref[...] = (0.5 + 0.5 * half_turn - target_ref[...]) * slope

    def weigh(group, slot):
        for j in range(2):
            rows = slice(j * TILE, (j + 1) * TILE)
            weight = weight_ref[...]
            back_re = field_ref[2 * group + j, :TILE] * weight
            back_im = field_ref[2 * group + j, TILE:] * weight
            back_refs[slot][rows, :TILE] = back_re.astype(jnp.bfloat16)
            back_refs[slot][rows, TILE:] = back_im.astype(jnp.bfloat16)

    def contract(group, slot):
        for j in range(2):
            rows = slice(j * TILE, (j + 1) * TILE)
            wave = dot(back_refs[slot][rows], bwd_ref[...])
            wave_refs[slot][rows] = wave.astype(jnp.bfloat16)

    def respond(group, slot):
        adj_re, adj_im = adj_ref[0], adj_ref[1]
        for j in range(2):
            resp = dot(inner_ref[...], wave_refs[slot][j * TILE : (j + 1) * TILE])
            resp_re = resp[:FREQ, :FREQ] + resp[FREQ:, FREQ:]
            resp_im = resp[:FREQ, FREQ:] - resp[FREQ:, :FREQ]
            kern_re, kern_im = kern_ref[0, 2 * group + j], kern_ref[1, 2 * group + j]
            adj_re = adj_re + (kern_re * resp_re + kern_im * resp_im)
            adj_im = adj_im + (kern_re * resp_im - kern_im * resp_re)
        adj_ref[0], adj_ref[1] = adj_re, adj_im

    adj_ref[...] = jnp.zeros_like(adj_ref)
    pipeline(groups, weigh, contract, respond)

    adj = jnp.concatenate([adj_ref[0] / PERIOD, adj_ref[1] / PERIOD], axis=1).astype(jnp.bfloat16)
    margin = dot(adj, margin_ref[...])
    left, right = pack(margin[:, :FREQ], margin[:, FREQ:])
    route("col", left.astype(jnp.bfloat16), right.astype(jnp.bfloat16), to_a_ref, to_b_ref)
    out_ref[...] = adj


def widen_kernel(adj_ref, fwd_ref, out_ref):
    wide = dot(adj_ref[...], fwd_ref[...])
    out_ref[:FREQ] = wide[:, :TILE]
    out_ref[FREQ:] = wide[:, TILE:]


def fold_kernel(wide_ref, from_a_ref, from_b_ref, patch_ref, out_ref, to_a_ref, to_b_ref):
    from_left, from_right = arrived("col", from_a_ref, from_b_ref)
    from_left, from_right = from_left.astype(jnp.float32), from_right.astype(jnp.float32)
    low, zero = low_lanes(FREQ), jnp.zeros((FREQ, 128), jnp.float32)
    turned_left, turned_right = pltpu.roll(from_left, 64, 1), pltpu.roll(from_right, 64, 1)
    first_half, second_half = slice(0, FREQ), slice(FREQ, 2 * FREQ)
    for half, left, right in (
        (first_half, turned_left, turned_right),
        (second_half, from_left, from_right),
    ):
        added = wide_ref[half, :128] + jnp.where(low, left, zero)
        out_ref[half, :128] = added.astype(jnp.bfloat16)
        added = wide_ref[half, 128:] + jnp.where(low, zero, right)
        out_ref[half, 128:] = added.astype(jnp.bfloat16)
    wide = out_ref[...]
    top = dot(patch_ref[:MARGIN], wide).astype(jnp.bfloat16)
    bottom = dot(patch_ref[MARGIN + TILE :], wide).astype(jnp.bfloat16)
    route("row", top, bottom, to_a_ref, to_b_ref)


def core_kernel(wide_ref, patch_ref, mask_ref, out_ref, rim_ref, rate_ref, rows_ref, sem):
    wide = wide_ref[...]
    ends = (slice(0, MARGIN), slice(MARGIN, TILE - MARGIN), slice(TILE - MARGIN, TILE))
    for i, rows in enumerate(ends):
        shifted = slice(rows.start + MARGIN, rows.stop + MARGIN)
        mask = mask_ref[rows]
        squashed = jax.nn.sigmoid(STEEPNESS * mask)
        rate = STEP_RATE * (2.0 * STEEPNESS) * squashed * (1.0 - squashed)
        updated = mask - dot(patch_ref[shifted], wide) * rate
        if i == 1:
            rows_ref[...] = updated
        else:
            rim_ref[i // 2], rate_ref[i // 2] = updated, rate
    copy = pltpu.make_async_copy(rows_ref, out_ref.at[pl.ds(MARGIN, TILE - 2 * MARGIN)], sem)
    copy.start()
    copy.wait()


def finish_kernel(most_ref, rim_ref, rate_ref, from_a_ref, from_b_ref, out_ref, rows_ref, sems):
    del most_ref
    copies = []
    for i, strip in enumerate(arrived("row", from_a_ref, from_b_ref)):
        rows_ref[i] = rim_ref[i] - strip.astype(jnp.float32) * rate_ref[i]
        start = i * (TILE - MARGIN)
        copy = pltpu.make_async_copy(rows_ref.at[i], out_ref.at[pl.ds(start, MARGIN)], sems.at[i])
        copy.start()
        copies.append(copy)
    for copy in copies:
        copy.wait()


def pairings(mesh):
    wins, rows, cols = (mesh.shape[axis] for axis in AXES)

    def flat(win, row, col):
        return (win * rows + row) * cols + col

    def row_b(win, row, col):
        other = row + 1 if row % 2 else row - 1
        return (win, other, col) if 0 <= other < rows else (win, row, col ^ 1)

    partners = dict(
        row_a=lambda w, r, c: (w, r ^ 1, c),
        row_b=row_b,
        col_a=lambda w, r, c: (w, r, c ^ 1),
        col_b=lambda w, r, c: (w, r, (c + 1 if c % 2 else c - 1) % cols),
    )
    places = [(w, r, c) for w in range(wins) for r in range(rows) for c in range(cols)]
    return {
        name: [(flat(*place), flat(*partner(*place))) for place in places]
        for name, partner in partners.items()
    }


def solution(mesh):
    assert mesh.shape["row"] % 2 == 0 and mesh.shape["col"] % 2 == 0
    pairs = pairings(mesh)
    tables = table_constants()
    bf16, f32 = jnp.bfloat16, jnp.float32
    shape = jax.ShapeDtypeStruct
    edge, strip = shape((MARGIN, TILE), bf16), shape((FREQ, 128), bf16)
    whole = shape((TILE, TILE), f32)
    dma = pltpu.SemaphoreType.DMA

    def swap(axis, to_a, to_b):
        return (
            lax.ppermute(to_a, AXES, pairs[axis + "_a"]),
            lax.ppermute(to_b, AXES, pairs[axis + "_b"]),
        )

    def local(mask_params, layout, kernels):
        edges = call(
            edges_kernel, (edge, edge), (mask_params,), 2 * MIB, "edges", hbm=(0,),
            scratch=(pltpu.VMEM((2, MARGIN, TILE), f32), dma((2 * PIECES,))),
        )
        inner, *others = (jnp.asarray(table) for table in tables.values())
        arrays = [inner, *others, jnp.transpose(kernels, (0, 2, 1, 3))]
        target, rows, *held, kern = call(
            functools.partial(prepare_kernel, len(arrays)),
            (whole, whole, *(shape(array.shape, array.dtype) for array in arrays)),
            (mask_params, layout[0, 0], *arrays),
            8 * MIB,
            "prepare",
            hbm=range(len(arrays) + 2),
            scratch=(
                pltpu.VMEM((TILE, TILE), f32),
                pltpu.VMEM(layout.shape[2:], jnp.int32),
                dma((len(arrays) + 2,)),
            ),
            flops=1_000_000_000,
            moved=3_000_000,
        )
        held = dict(zip(tables, held))
        rows, *strips = call(
            strips_kernel,
            (shape((2 * FREQ, TILE), bf16), strip, strip),
            (rows, *swap("row", *edges), held["rim"]),
            2 * MIB,
            "strips",
        )
        (inside,) = call(
            inside_kernel, (whole,), (rows, held["patch"]), 2 * MIB, "inside",
            flops=100_000_000, moved=600_000,
        )
        *strips, adj = call(
            tile_kernel,
            (strip, strip, shape((FREQ, 2 * FREQ), bf16)),
            (inside, *swap("col", *strips), target, kern, *held.values()),
            32 * MIB,
            "tile",
            scratch=(
                pltpu.VMEM((KERNELS, 2 * TILE, TILE), f32),
                pltpu.VMEM((TILE, TILE), f32),
                pltpu.VMEM((TILE, TILE), f32),
                pltpu.VMEM((2, FREQ, FREQ), f32),
                pltpu.VMEM((2, FREQ, FREQ), f32),
                *[pltpu.VMEM((2 * FREQ, 2 * FREQ), bf16)] * 2,
                *[pltpu.VMEM((2, 2 * FREQ, TILE), bf16)] * 2,
                *[pltpu.VMEM((2 * TILE, 2 * TILE), bf16)] * 2,
                *[pltpu.VMEM((2 * TILE, 2 * FREQ), bf16)] * 2,
            ),
            flops=2_500_000_000,
            moved=8_000_000,
        )
        (wide,) = call(
            widen_kernel, (whole,), (adj, held["fwd"]), 2 * MIB, "widen",
            flops=100_000_000, moved=600_000,
        )
        wide, *edges = call(
            fold_kernel,
            (shape((2 * FREQ, TILE), bf16), edge, edge),
            (wide, *swap("col", *strips), held["patch"]),
            4 * MIB,
            "fold",
        )
        ends = shape((2, MARGIN, TILE), f32)
        most, rim, rate = call(
            core_kernel,
            (whole, ends, ends),
            (wide, held["patch"], mask_params),
            4 * MIB,
            "core",
            hbm_out=(0,),
            scratch=(pltpu.VMEM((TILE - 2 * MARGIN, TILE), f32), dma(())),
            flops=200_000_000,
            moved=1_000_000,
        )
        (updated,) = call(
            finish_kernel,
            (whole,),
            (most, rim, rate, *swap("row", *edges)),
            4 * MIB,
            "finish",
            hbm=(0,),
            hbm_out=(0,),
            scratch=(pltpu.VMEM((2, MARGIN, TILE), f32), dma((2,))),
            input_output_aliases={0: 0},
        )
        return updated

    in_specs = (P(("win", "row"), "col"), P(("win", "row"), "col", None, None), P())
    out_specs = P(("win", "row"), "col")
    return jax.shard_map(local, mesh=mesh, in_specs=in_specs, out_specs=out_specs, check_vma=False)
```

```python
import functools
import math

import jax
import jax.numpy as jnp
import ml_dtypes
import numpy as np
from jax import lax
from jax.experimental import pallas as pl
from jax.experimental.pallas import tpu as pltpu
from jax.sharding import PartitionSpec as P

TILE = 256
MARGIN = 64
PERIOD = 384
FREQ = 128
KERNELS = 12
STEEPNESS = 2.0
CONTRAST = 4.0
THRESHOLD = 0.75
STEP_RATE = 1.0

AXES = ("win", "row", "col")
MIB = 1 << 20


def table_constants():
    frequency = np.arange(FREQ, dtype=np.int64) - FREQ // 2
    places = np.arange(PERIOD, dtype=np.int64)
    angles = np.mod(frequency[:, None] * places[None, :], PERIOD) * (2.0 * math.pi / PERIOD)
    cos_t = np.cos(angles).astype(np.float32)
    sin_t = np.sin(angles).astype(np.float32)
    inner = np.arange(MARGIN, MARGIN + TILE)
    rim = np.concatenate([np.arange(MARGIN), np.arange(MARGIN + TILE, PERIOD)])
    ci, si, cm, sm = cos_t[:, inner], sin_t[:, inner], cos_t[:, rim], sin_t[:, rim]
    names = dict(
        inner=np.concatenate([ci, si], axis=0),
        rim=np.concatenate([cm, sm], axis=0),
        patch=np.concatenate([cos_t.T, -sin_t.T], axis=1),
        fwd=np.block([[ci, si], [-si, ci]]),
        bwd=np.block([[ci.T, -si.T], [si.T, ci.T]]),
        margin=np.block([[cm, sm], [-sm, cm]]),
    )
    return {name: value.astype(ml_dtypes.bfloat16) for name, value in names.items()}


def dot(left, right):
    return jnp.dot(left, right, preferred_element_type=jnp.float32)


VMEM = pl.BlockSpec(memory_space=pltpu.VMEM)
HBM = pl.BlockSpec(memory_space=pltpu.HBM)


def call(kernel, outs, args, limit, name, scratch=(), flops=0, moved=0, hbm=(), hbm_out=(), flags=None, **more):
    args = [
        pltpu.with_memory_space_constraint(arg, pltpu.HBM) if i in hbm else arg
        for i, arg in enumerate(args)
    ]
    return pl.pallas_call(
        kernel,
        out_shape=outs,
        in_specs=[HBM if i in hbm else VMEM for i in range(len(args))],
        out_specs=tuple(HBM if i in hbm_out else VMEM for i in range(len(outs))),
        scratch_shapes=list(scratch),
        compiler_params=pltpu.CompilerParams(vmem_limit_bytes=limit, flags=flags),
        cost_estimate=pl.CostEstimate(flops=flops, bytes_accessed=moved, transcendentals=0),
        name=name,
        **more,
    )(*args)


def first_is_ahead(axis):
    return lax.rem(lax.axis_index(axis), 2) == (0 if axis == "row" else 1)


def route(axis, back, ahead, to_a_ref, to_b_ref):
    ahead_first = first_is_ahead(axis)
    to_a_ref[...] = jnp.where(ahead_first, ahead, back)
    to_b_ref[...] = jnp.where(ahead_first, back, ahead)


def arrived(axis, from_a_ref, from_b_ref):
    ahead_first, at, size = first_is_ahead(axis), lax.axis_index(axis), lax.axis_size(axis)
    a, b = from_a_ref[...], from_b_ref[...]
    zero = jnp.zeros_like(a)
    before = jnp.where(at == 0, zero, jnp.where(ahead_first, b, a))
    after = jnp.where(at == size - 1, zero, jnp.where(ahead_first, a, b))
    return before, after


def low_lanes(rows):
    return lax.broadcasted_iota(jnp.int32, (rows, 128), 1) < 64


def pack(first, second):
    low, turned = low_lanes(FREQ), pltpu.roll(second, 64, 1)
    return jnp.where(low, first, turned), jnp.where(low, turned, first)


def to_transmit(mask):
    return (2.0 * jax.nn.sigmoid(STEEPNESS * mask) - 1.0).astype(jnp.bfloat16)


def edges_kernel(mask_ref, to_a_ref, to_b_ref, rows_ref, sems):
    starts = (0, TILE - MARGIN)
    copies = fetch(
        [(mask_ref.at[pl.ds(start, MARGIN)], rows_ref.at[i]) for i, start in enumerate(starts)],
        sems,
    )
    for copy in copies:
        copy.wait()
    route("row", to_transmit(rows_ref[0]), to_transmit(rows_ref[1]), to_a_ref, to_b_ref)


def fetch(moves, sems):
    copies = [
        pltpu.make_async_copy(source, dest, sems.at[i]) for i, (source, dest) in enumerate(moves)
    ]
    for copy in copies:
        copy.start()
    return copies


def prepare_kernel(
    mask_ref, rect_ref, inner_ref, rim_ref, patch_ref, kern_ref,
    target_ref, rows_ref, to_inner_ref, to_rim_ref, to_patch_ref, to_kern_ref,
    mask_buf, rect_buf, sems,
):
    rects_in, mask_in, inner_in, *others = fetch(
        (
            (rect_ref, rect_buf),
            (mask_ref, mask_buf),
            (inner_ref, to_inner_ref),
            (rim_ref, to_rim_ref),
            (patch_ref, to_patch_ref),
            (kern_ref.at[0], to_kern_ref),
        ),
        sems,
    )
    rects_in.wait()
    rects = rect_buf[...]
    places = lax.broadcasted_iota(jnp.int32, (TILE, rects.shape[1]), 0)
    row_in = ((places >= rects[0:1]) & (places < rects[1:2])).astype(jnp.bfloat16)
    col_in = ((places >= rects[2:3]) & (places < rects[3:4])).astype(jnp.bfloat16)
    covered = lax.dot_general(
        row_in, col_in, (((1,), (1,)), ((), ())), preferred_element_type=jnp.float32
    )
    target_ref[...] = jnp.minimum(covered, 1.0)
    mask_in.wait()
    transmit = to_transmit(mask_buf[...])
    inner_in.wait()
    rows_ref[...] = dot(to_inner_ref[...], transmit)
    for copy in others:
        copy.wait()


def strips_kernel(rows_ref, from_a_ref, from_b_ref, rim_ref, out_ref, to_a_ref, to_b_ref):
    above, below = arrived("row", from_a_ref, from_b_ref)
    halo = jnp.concatenate([above, below], axis=0)
    parts = []
    for half in (slice(0, FREQ), slice(FREQ, 2 * FREQ)):
        part = (rows_ref[half] + dot(rim_ref[half], halo)).astype(jnp.bfloat16)
        out_ref[half] = part
        parts.append(part)
    low = low_lanes(FREQ)
    first, second = (jnp.where(low, part[:, :128], part[:, 128:]) for part in parts)
    left, right = pack(first, second)
    route("col", left, right, to_a_ref, to_b_ref)


def inside_kernel(
    rows_ref, patch_ref, fwd_ref, bwd_ref, margin_ref, kern_ref,
    out_ref, to_fwd_ref, to_bwd_ref, to_margin_ref, to_kern_ref, sems,
):
    copies = fetch(
        (
            (fwd_ref, to_fwd_ref),
            (bwd_ref, to_bwd_ref),
            (margin_ref, to_margin_ref),
            (kern_ref.at[1], to_kern_ref),
        ),
        sems,
    )
    for half in (slice(0, FREQ), slice(FREQ, 2 * FREQ)):
        out_ref[half] = dot(rows_ref[half], patch_ref[MARGIN : MARGIN + TILE])
    for copy in copies:
        copy.wait()


def pipeline(groups, first, second, third):
    def step(at, parity):
        static = isinstance(at, int)
        if not static or -1 <= at < groups - 1:
            second(at + 1, 1 - parity)
        if not static or at >= 0:
            third(at, parity)
        if not static or at < groups - 2:
            first(at + 2, parity)

    for at in range(-2, groups):
        step(at, at % 2)


def tile_kernel(
    inside_ref, from_a_ref, from_b_ref, target_ref, kern_re_ref, kern_im_ref,
    inner_ref, patch_ref, fwd_ref, bwd_ref, margin_ref,
    to_a_ref, to_b_ref, out_ref,
    field_ref, bright_ref, weight_ref, spec_ref, adj_ref, *slot_refs,
):
    mixed_refs, line_refs, back_refs, wave_refs = (slot_refs[i : i + 2] for i in (0, 2, 4, 6))
    from_left, from_right = arrived("col", from_a_ref, from_b_ref)
    low = low_lanes(FREQ)
    head, tail = patch_ref[:MARGIN], patch_ref[MARGIN + TILE :]
    first = dot(jnp.where(low, from_right, from_left), jnp.concatenate([tail, head], axis=0))
    second = dot(jnp.where(low, from_left, from_right), jnp.concatenate([head, tail], axis=0))
    first, second = first + inside_ref[:FREQ], second + inside_ref[FREQ:]
    spec_re = (first[:, :FREQ] + second[:, FREQ:]) / PERIOD
    spec_im = (first[:, FREQ:] - second[:, :FREQ]) / PERIOD
    spec_ref[0], spec_ref[1] = spec_re, spec_im
    groups = KERNELS // 2

    def mix(group, slot):
        for j in range(2):
            k = 2 * group + j
            kern_re, kern_im = kern_re_ref[k], kern_im_ref[k]
            spec_re, spec_im = spec_ref[0], spec_ref[1]
            rows = slice(j * FREQ, (j + 1) * FREQ)
            mixed_re = kern_re * spec_re - kern_im * spec_im
            mixed_im = kern_re * spec_im + kern_im * spec_re
            mixed_refs[slot][rows, :FREQ] = mixed_re.astype(jnp.bfloat16)
            mixed_refs[slot][rows, FREQ:] = mixed_im.astype(jnp.bfloat16)

    def expand(group, slot):
        line = dot(mixed_refs[slot][...], fwd_ref[...]).astype(jnp.bfloat16)
        for j in range(2):
            rows = slice(j * FREQ, (j + 1) * FREQ)
            line_refs[slot][j, :FREQ] = line[rows, :TILE]
            line_refs[slot][j, FREQ:] = line[rows, TILE:]

    def image(group, slot):
        total = bright_ref[...]
        for j in range(2):
            field = dot(bwd_ref[...], line_refs[slot][j])
            field_ref[2 * group + j] = field
            total = total + (field[:TILE] * field[:TILE] + field[TILE:] * field[TILE:])
        bright_ref[...] = total

    bright_ref[...] = jnp.zeros_like(bright_ref)
    pipeline(groups, mix, expand, image)

    half_turn = jnp.tanh(
        bright_ref[...] * (CONTRAST / (2.0 * KERNELS)) - CONTRAST * THRESHOLD / 2.0
    )
    slope = (2.0 * CONTRAST / 4.0) * (2.0 / KERNELS) * (1.0 - half_turn * half_turn)
    weight_ref[...] = (0.5 + 0.5 * half_turn - target_ref[...]) * slope

    def weigh(group, slot):
        for j in range(2):
            rows = slice(j * TILE, (j + 1) * TILE)
            weight = weight_ref[...]
            back_re = field_ref[2 * group + j, :TILE] * weight
            back_im = field_ref[2 * group + j, TILE:] * weight
            back_refs[slot][rows, :TILE] = back_re.astype(jnp.bfloat16)
            back_refs[slot][rows, TILE:] = back_im.astype(jnp.bfloat16)

    def contract(group, slot):
        for j in range(2):
            rows = slice(j * TILE, (j + 1) * TILE)
            wave = dot(back_refs[slot][rows], bwd_ref[...])
            wave_refs[slot][rows] = wave.astype(jnp.bfloat16)

    def respond(group, slot):
        adj_re, adj_im = adj_ref[0], adj_ref[1]
        for j in range(2):
            resp = dot(inner_ref[...], wave_refs[slot][j * TILE : (j + 1) * TILE])
            resp_re = resp[:FREQ, :FREQ] + resp[FREQ:, FREQ:]
            resp_im = resp[:FREQ, FREQ:] - resp[FREQ:, :FREQ]
            kern_re, kern_im = kern_re_ref[2 * group + j], kern_im_ref[2 * group + j]
            adj_re = adj_re + (kern_re * resp_re + kern_im * resp_im)
            adj_im = adj_im + (kern_re * resp_im - kern_im * resp_re)
        adj_ref[0], adj_ref[1] = adj_re, adj_im

    adj_ref[...] = jnp.zeros_like(adj_ref)
    pipeline(groups, weigh, contract, respond)

    adj = jnp.concatenate([adj_ref[0] / PERIOD, adj_ref[1] / PERIOD], axis=1).astype(jnp.bfloat16)
    margin = dot(adj, margin_ref[...])
    left, right = pack(margin[:, :FREQ], margin[:, FREQ:])
    route("col", left.astype(jnp.bfloat16), right.astype(jnp.bfloat16), to_a_ref, to_b_ref)
    out_ref[...] = adj


def widen_kernel(adj_ref, fwd_ref, out_ref):
    wide = dot(adj_ref[...], fwd_ref[...])
    out_ref[:FREQ] = wide[:, :TILE]
    out_ref[FREQ:] = wide[:, TILE:]


def fold_kernel(wide_ref, from_a_ref, from_b_ref, patch_ref, out_ref, to_a_ref, to_b_ref):
    from_left, from_right = arrived("col", from_a_ref, from_b_ref)
    from_left, from_right = from_left.astype(jnp.float32), from_right.astype(jnp.float32)
    low, zero = low_lanes(FREQ), jnp.zeros((FREQ, 128), jnp.float32)
    turned_left, turned_right = pltpu.roll(from_left, 64, 1), pltpu.roll(from_right, 64, 1)
    first_half, second_half = slice(0, FREQ), slice(FREQ, 2 * FREQ)
    for half, left, right in (
        (first_half, turned_left, turned_right),
        (second_half, from_left, from_right),
    ):
        added = wide_ref[half, :128] + jnp.where(low, left, zero)
        out_ref[half, :128] = added.astype(jnp.bfloat16)
        added = wide_ref[half, 128:] + jnp.where(low, zero, right)
        out_ref[half, 128:] = added.astype(jnp.bfloat16)
    wide = out_ref[...]
    top = dot(patch_ref[:MARGIN], wide).astype(jnp.bfloat16)
    bottom = dot(patch_ref[MARGIN + TILE :], wide).astype(jnp.bfloat16)
    route("row", top, bottom, to_a_ref, to_b_ref)


def core_kernel(wide_ref, patch_ref, mask_ref, out_ref, rim_ref, rate_ref, rows_ref, sem):
    wide = wide_ref[...]
    ends = (slice(0, MARGIN), slice(MARGIN, TILE - MARGIN), slice(TILE - MARGIN, TILE))
    for i, rows in enumerate(ends):
        shifted = slice(rows.start + MARGIN, rows.stop + MARGIN)
        mask = mask_ref[rows]
        squashed = jax.nn.sigmoid(STEEPNESS * mask)
        rate = STEP_RATE * (2.0 * STEEPNESS) * squashed * (1.0 - squashed)
        updated = mask - dot(patch_ref[shifted], wide) * rate
        if i == 1:
            rows_ref[...] = updated
        else:
            rim_ref[i // 2], rate_ref[i // 2] = updated, rate
    copy = pltpu.make_async_copy(rows_ref, out_ref.at[pl.ds(MARGIN, TILE - 2 * MARGIN)], sem)
    copy.start()
    copy.wait()


def finish_kernel(most_ref, rim_ref, rate_ref, from_a_ref, from_b_ref, out_ref, rows_ref, sems):
    del most_ref
    copies = []
    for i, strip in enumerate(arrived("row", from_a_ref, from_b_ref)):
        rows_ref[i] = rim_ref[i] - strip.astype(jnp.float32) * rate_ref[i]
        start = i * (TILE - MARGIN)
        copy = pltpu.make_async_copy(rows_ref.at[i], out_ref.at[pl.ds(start, MARGIN)], sems.at[i])
        copy.start()
        copies.append(copy)
    for copy in copies:
        copy.wait()


def pairings(mesh):
    wins, rows, cols = (mesh.shape[axis] for axis in AXES)

    def flat(win, row, col):
        return (win * rows + row) * cols + col

    def row_b(win, row, col):
        other = row + 1 if row % 2 else row - 1
        return (win, other, col) if 0 <= other < rows else (win, row, col ^ 1)

    partners = dict(
        row_a=lambda w, r, c: (w, r ^ 1, c),
        row_b=row_b,
        col_b=lambda w, r, c: (w, r, c ^ 1),
        col_a=lambda w, r, c: (w, r, (c + 1 if c % 2 else c - 1) % cols),
    )
    places = [(w, r, c) for w in range(wins) for r in range(rows) for c in range(cols)]
    return {
        name: [(flat(*place), flat(*partner(*place))) for place in places]
        for name, partner in partners.items()
    }


def solution(mesh):
    assert mesh.shape["row"] % 2 == 0 and mesh.shape["col"] % 2 == 0
    pairs = pairings(mesh)
    tables = table_constants()
    bf16, f32 = jnp.bfloat16, jnp.float32
    shape = jax.ShapeDtypeStruct
    edge, strip = shape((MARGIN, TILE), bf16), shape((FREQ, 128), bf16)
    whole = shape((TILE, TILE), f32)
    dma = pltpu.SemaphoreType.DMA

    def swap(axis, to_a, to_b):
        return (
            lax.ppermute(to_a, AXES, pairs[axis + "_a"]),
            lax.ppermute(to_b, AXES, pairs[axis + "_b"]),
        )

    def local(mask_params, layout, kernels):
        edges = call(
            edges_kernel, (edge, edge), (mask_params,), 2 * MIB, "edges", hbm=(0,),
            scratch=(pltpu.VMEM((2, MARGIN, TILE), f32), dma((2,))),
        )
        kern = jnp.transpose(kernels, (0, 2, 1, 3))
        part = shape(kern.shape[1:], f32)

        def like(*arrays):
            return tuple(shape(array.shape, array.dtype) for array in arrays)

        inner, rim, patch, fwd, bwd, margin = (jnp.asarray(table) for table in tables.values())
        target, rows, inner, rim, patch, kern_re = call(
            prepare_kernel,
            (whole, whole, *like(inner, rim, patch), part),
            (mask_params, layout[0, 0], inner, rim, patch, kern),
            8 * MIB,
            "prepare",
            hbm=range(6),
            scratch=(
                pltpu.VMEM((TILE, TILE), f32),
                pltpu.VMEM(layout.shape[2:], jnp.int32),
                dma((6,)),
            ),
            flops=1_000_000_000,
            moved=1_500_000,
        )
        rows, *strips = call(
            strips_kernel,
            (shape((2 * FREQ, TILE), bf16), strip, strip),
            (rows, *swap("row", *edges), rim),
            2 * MIB,
            "strips",
        )
        inside, fwd, bwd, margin, kern_im = call(
            inside_kernel,
            (whole, *like(fwd, bwd, margin), part),
            (rows, patch, fwd, bwd, margin, kern),
            8 * MIB,
            "inside",
            hbm=range(2, 6),
            scratch=(dma((4,)),),
            flops=1_000_000_000,
            moved=1_500_000,
        )
        *strips, adj = call(
            tile_kernel,
            (strip, strip, shape((FREQ, 2 * FREQ), bf16)),
            (
                inside,
                *swap("col", *strips),
                target,
                kern_re,
                kern_im,
                inner,
                patch,
                fwd,
                bwd,
                margin,
            ),
            32 * MIB,
            "tile",
            scratch=(
                pltpu.VMEM((KERNELS, 2 * TILE, TILE), f32),
                pltpu.VMEM((TILE, TILE), f32),
                pltpu.VMEM((TILE, TILE), f32),
                pltpu.VMEM((2, FREQ, FREQ), f32),
                pltpu.VMEM((2, FREQ, FREQ), f32),
                *[pltpu.VMEM((2 * FREQ, 2 * FREQ), bf16)] * 2,
                *[pltpu.VMEM((2, 2 * FREQ, TILE), bf16)] * 2,
                *[pltpu.VMEM((2 * TILE, 2 * TILE), bf16)] * 2,
                *[pltpu.VMEM((2 * TILE, 2 * FREQ), bf16)] * 2,
            ),
            flops=2_500_000_000,
            moved=8_000_000,
        )
        (wide,) = call(
            widen_kernel, (whole,), (adj, fwd), 2 * MIB, "widen",
            flops=100_000_000, moved=600_000,
        )
        wide, *edges = call(
            fold_kernel,
            (shape((2 * FREQ, TILE), bf16), edge, edge),
            (wide, *swap("col", *strips), patch),
            4 * MIB,
            "fold",
        )
        ends = shape((2, MARGIN, TILE), f32)
        most, rim, rate = call(
            core_kernel,
            (whole, ends, ends),
            (wide, patch, mask_params),
            4 * MIB,
            "core",
            hbm_out=(0,),
            scratch=(pltpu.VMEM((TILE - 2 * MARGIN, TILE), f32), dma(())),
            flops=200_000_000,
            moved=1_000_000,
        )
        (updated,) = call(
            finish_kernel,
            (whole,),
            (most, rim, rate, *swap("row", *edges)),
            4 * MIB,
            "finish",
            hbm=(0,),
            hbm_out=(0,),
            scratch=(pltpu.VMEM((2, MARGIN, TILE), f32), dma((2,))),
            input_output_aliases={0: 0},
        )
        return updated

    in_specs = (P(("win", "row"), "col"), P(("win", "row"), "col", None, None), P())
    out_specs = P(("win", "row"), "col")
    return jax.shard_map(local, mesh=mesh, in_specs=in_specs, out_specs=out_specs, check_vma=False)
```

```python
import itertools
import math

import jax
import jax.numpy as jnp
import ml_dtypes
import numpy as np
from jax import lax
from jax.experimental import pallas as pl
from jax.experimental.pallas import tpu as pltpu
from jax.sharding import PartitionSpec as P

TILE = 256
MARGIN = 64
PERIOD = 384
FREQ = 128
KERNELS = 12
STEEPNESS = 2.0
CONTRAST = 4.0
THRESHOLD = 0.75
STEP_RATE = 1.0

AXES = ("win", "row", "col")
MIB = 1 << 20
BLOCK = 64
TURNED = {"row1": (0, 0), "col1": (1, 1), "col2": (1, 1), "row2": (0, 0)}


def table_constants():
    frequency = np.arange(FREQ, dtype=np.int64) - FREQ // 2
    places = np.arange(PERIOD, dtype=np.int64)
    angles = np.mod(frequency[:, None] * places[None, :], PERIOD) * (2.0 * math.pi / PERIOD)
    cos_t = np.cos(angles).astype(np.float32)
    sin_t = np.sin(angles).astype(np.float32)
    inner = np.arange(MARGIN, MARGIN + TILE)
    rim = np.concatenate([np.arange(MARGIN), np.arange(MARGIN + TILE, PERIOD)])
    ci, si, cm, sm = cos_t[:, inner], sin_t[:, inner], cos_t[:, rim], sin_t[:, rim]
    names = dict(
        inner=np.concatenate([ci, si], axis=0),
        rim=np.concatenate([cm, sm], axis=0),
        patch=np.concatenate([cos_t.T, -sin_t.T], axis=1),
        fwd=np.block([[ci, si], [-si, ci]]),
        bwd=np.block([[ci.T, -si.T], [si.T, ci.T]]),
        margin=np.block([[cm, sm], [-sm, cm]]),
    )
    names["image"] = names["bwd"].reshape(2, TILE // BLOCK, BLOCK, -1).swapaxes(0, 1).reshape(2 * TILE, -1)
    return {name: value.astype(ml_dtypes.bfloat16) for name, value in names.items()}


def dot(left, right):
    return jnp.dot(left, right, preferred_element_type=jnp.float32)


VMEM = pl.BlockSpec(memory_space=pltpu.VMEM)
HBM = pl.BlockSpec(memory_space=pltpu.HBM)


def call(kernel, outs, args, limit, name, scratch=(), flops=0, moved=0, hbm=(), hbm_out=(), flags=None, **more):
    args = [
        pltpu.with_memory_space_constraint(arg, pltpu.HBM) if i in hbm else arg
        for i, arg in enumerate(args)
    ]
    return pl.pallas_call(
        kernel,
        out_shape=outs,
        in_specs=[HBM if i in hbm else VMEM for i in range(len(args))],
        out_specs=tuple(HBM if i in hbm_out else VMEM for i in range(len(outs))),
        scratch_shapes=list(scratch),
        compiler_params=pltpu.CompilerParams(vmem_limit_bytes=limit, flags=flags),
        cost_estimate=pl.CostEstimate(flops=flops, bytes_accessed=moved, transcendentals=0),
        name=name,
        **more,
    )(*args)


def first_is_ahead(phase):
    turned = jnp.where(lax.rem(lax.axis_index("win"), 2) == 0, *TURNED[phase])
    return lax.rem(lax.axis_index(phase[:3]) + turned, 2) == 0


def route(phase, back, ahead, to_a_ref, to_b_ref):
    ahead_first = first_is_ahead(phase)
    to_a_ref[...] = jnp.where(ahead_first, ahead, back)
    to_b_ref[...] = jnp.where(ahead_first, back, ahead)


def arrived(phase, from_a_ref, from_b_ref):
    axis = phase[:3]
    ahead_first, at, size = first_is_ahead(phase), lax.axis_index(axis), lax.axis_size(axis)
    a, b = from_a_ref[...], from_b_ref[...]
    zero = jnp.zeros_like(a)
    before = jnp.where(at == 0, zero, jnp.where(ahead_first, b, a))
    after = jnp.where(at == size - 1, zero, jnp.where(ahead_first, a, b))
    return before, after


def low_lanes(rows):
    return lax.broadcasted_iota(jnp.int32, (rows, 128), 1) < 64


def pack(first, second):
    low, turned = low_lanes(FREQ), pltpu.roll(second, 64, 1)
    return jnp.where(low, first, turned), jnp.where(low, turned, first)


def to_transmit(mask):
    return (2.0 * jax.nn.sigmoid(STEEPNESS * mask) - 1.0).astype(jnp.bfloat16)


def edges_kernel(mask_ref, to_a_ref, to_b_ref, rows_ref, sems):
    starts = (0, TILE - MARGIN)
    copies = fetch(
        [(mask_ref.at[pl.ds(start, MARGIN)], rows_ref.at[i]) for i, start in enumerate(starts)],
        sems,
    )
    for copy in copies:
        copy.wait()
    route("row1", to_transmit(rows_ref[0]), to_transmit(rows_ref[1]), to_a_ref, to_b_ref)


def fetch(moves, sems):
    copies = [
        pltpu.make_async_copy(source, dest, sems.at[i]) for i, (source, dest) in enumerate(moves)
    ]
    for copy in copies:
        copy.start()
    return copies


def prepare_kernel(
    mask_ref, rect_ref, inner_ref, rim_ref, patch_ref, fwd_ref, kern_ref,
    level_ref, rows_ref, to_inner_ref, to_rim_ref, to_patch_ref, to_fwd_ref, to_kern_ref,
    mask_buf, rect_buf, sems,
):
    rects_in, mask_in, inner_in, *others = fetch(
        (
            (rect_ref, rect_buf),
            (mask_ref, mask_buf),
            (inner_ref, to_inner_ref),
            (rim_ref, to_rim_ref),
            (patch_ref, to_patch_ref),
            (fwd_ref, to_fwd_ref),
            (kern_ref.at[0], to_kern_ref),
        ),
        sems,
    )
    rects_in.wait()
    rects = rect_buf[...]
    places = lax.broadcasted_iota(jnp.int32, (TILE, rects.shape[1]), 0)
    row_in = ((places >= rects[0:1]) & (places < rects[1:2])).astype(jnp.bfloat16)
    col_in = ((places >= rects[2:3]) & (places < rects[3:4])).astype(jnp.bfloat16)
    covered = lax.dot_general(
        row_in, col_in, (((1,), (1,)), ((), ())), preferred_element_type=jnp.float32
    )
    level_ref[...] = 1.0 - 2.0 * jnp.minimum(covered, 1.0)
    mask_in.wait()
    transmit = to_transmit(mask_buf[...])
    inner_in.wait()
    rows_ref[...] = dot(to_inner_ref[...], transmit)
    for copy in others:
        copy.wait()


def strips_kernel(rows_ref, from_a_ref, from_b_ref, rim_ref, out_ref, to_a_ref, to_b_ref):
    above, below = arrived("row1", from_a_ref, from_b_ref)
    halo = jnp.concatenate([above, below], axis=0)
    parts = []
    for half in (slice(0, FREQ), slice(FREQ, 2 * FREQ)):
        part = (rows_ref[half] + dot(rim_ref[half], halo)).astype(jnp.bfloat16)
        out_ref[half] = part
        parts.append(part)
    low = low_lanes(FREQ)
    first, second = (jnp.where(low, part[:, :128], part[:, 128:]) for part in parts)
    left, right = pack(first, second)
    route("col1", left, right, to_a_ref, to_b_ref)


def inside_kernel(
    rows_ref, patch_ref, bwd_ref, margin_ref, image_ref, kern_ref,
    out_ref, to_bwd_ref, to_margin_ref, to_image_ref, to_kern_ref, sems,
):
    copies = fetch(
        (
            (bwd_ref, to_bwd_ref),
            (margin_ref, to_margin_ref),
            (image_ref, to_image_ref),
            (kern_ref.at[1], to_kern_ref),
        ),
        sems,
    )
    for half in (slice(0, FREQ), slice(FREQ, 2 * FREQ)):
        out_ref[half] = dot(rows_ref[half], patch_ref[MARGIN : MARGIN + TILE])
    for copy in copies:
        copy.wait()


def pipeline(groups, first, second, third):
    def step(at, parity):
        static = isinstance(at, int)
        if not static or -1 <= at < groups - 1:
            second(at + 1, 1 - parity)
        if not static or at >= 0:
            third(at, parity)
        if not static or at < groups - 2:
            first(at + 2, parity)

    for at in range(-2, groups):
        step(at, at % 2)


def tile_kernel(
    inside_ref, from_a_ref, from_b_ref, level_ref, kern_re_ref, kern_im_ref,
    inner_ref, patch_ref, fwd_ref, bwd_ref, margin_ref, image_ref,
    to_a_ref, to_b_ref, out_ref,
    field_ref, bright_ref, weight_ref, spec_ref, adj_ref, *slot_refs,
):
    mixed_refs, line_refs, back_refs, wave_refs = (slot_refs[i : i + 2] for i in (0, 2, 4, 6))
    from_left, from_right = arrived("col1", from_a_ref, from_b_ref)
    low = low_lanes(FREQ)
    head, tail = patch_ref[:MARGIN], patch_ref[MARGIN + TILE :]
    first = dot(jnp.where(low, from_right, from_left), jnp.concatenate([tail, head], axis=0))
    second = dot(jnp.where(low, from_left, from_right), jnp.concatenate([head, tail], axis=0))
    first, second = first + inside_ref[:FREQ], second + inside_ref[FREQ:]
    spec_re = (first[:, :FREQ] + second[:, FREQ:]) / PERIOD
    spec_im = (first[:, FREQ:] - second[:, :FREQ]) / PERIOD
    spec_ref[0], spec_ref[1] = spec_re, spec_im
    groups = KERNELS // 2

    def mix(group, slot):
        for j in range(2):
            k = 2 * group + j
            kern_re, kern_im = kern_re_ref[k], kern_im_ref[k]
            spec_re, spec_im = spec_ref[0], spec_ref[1]
            rows = slice(j * FREQ, (j + 1) * FREQ)
            mixed_re = kern_re * spec_re - kern_im * spec_im
            mixed_im = kern_re * spec_im + kern_im * spec_re
            mixed_refs[slot][rows, :FREQ] = mixed_re.astype(jnp.bfloat16)
            mixed_refs[slot][rows, FREQ:] = mixed_im.astype(jnp.bfloat16)

    def expand(group, slot):
        line = dot(mixed_refs[slot][...], fwd_ref[...]).astype(jnp.bfloat16)
        for j in range(2):
            rows = slice(j * FREQ, (j + 1) * FREQ)
            line_refs[slot][j, :FREQ] = line[rows, :TILE]
            line_refs[slot][j, FREQ:] = line[rows, TILE:]

    def image(group, slot):
        fields = [dot(image_ref[...], line_refs[slot][j]) for j in range(2)]
        for at in range(0, TILE, BLOCK):
            rows = slice(at, at + BLOCK)
            total = bright_ref[rows]
            for j, field in enumerate(fields):
                field_re = field[2 * at : 2 * at + BLOCK]
                field_im = field[2 * at + BLOCK : 2 * at + 2 * BLOCK]
                field_ref[2 * group + j, rows] = field_re
                field_ref[2 * group + j, TILE + at : TILE + at + BLOCK] = field_im
                total = total + (field_re * field_re + field_im * field_im)
            bright_ref[rows] = total

    bright_ref[...] = jnp.zeros_like(bright_ref)
    pipeline(groups, mix, expand, image)

    turn = jnp.tanh(bright_ref[...] * (CONTRAST / (2.0 * KERNELS)) - CONTRAST * THRESHOLD / 2.0)
    weight_ref[...] = (turn + level_ref[...]) * (1.0 - turn * turn)

    def weigh(group, slot):
        for j in range(2):
            rows = slice(j * TILE, (j + 1) * TILE)
            weight = weight_ref[...]
            back_re = field_ref[2 * group + j, :TILE] * weight
            back_im = field_ref[2 * group + j, TILE:] * weight
            back_refs[slot][rows, :TILE] = back_re.astype(jnp.bfloat16)
            back_refs[slot][rows, TILE:] = back_im.astype(jnp.bfloat16)

    def contract(group, slot):
        for j in range(2):
            rows = slice(j * TILE, (j + 1) * TILE)
            wave = dot(back_refs[slot][rows], bwd_ref[...])
            wave_refs[slot][rows] = wave.astype(jnp.bfloat16)

    def respond(group, slot):
        adj_re, adj_im = adj_ref[0], adj_ref[1]
        for j in range(2):
            resp = dot(inner_ref[...], wave_refs[slot][j * TILE : (j + 1) * TILE])
            resp_re = resp[:FREQ, :FREQ] + resp[FREQ:, FREQ:]
            resp_im = resp[:FREQ, FREQ:] - resp[FREQ:, :FREQ]
            kern_re, kern_im = kern_re_ref[2 * group + j], kern_im_ref[2 * group + j]
            adj_re = adj_re + (kern_re * resp_re + kern_im * resp_im)
            adj_im = adj_im + (kern_re * resp_im - kern_im * resp_re)
        adj_ref[0], adj_ref[1] = adj_re, adj_im

    adj_ref[...] = jnp.zeros_like(adj_ref)
    pipeline(groups, weigh, contract, respond)

    scale = (CONTRAST / 4.0) * (2.0 / KERNELS) / PERIOD
    adj = (jnp.concatenate([adj_ref[0], adj_ref[1]], axis=1) * scale).astype(jnp.bfloat16)
    margin = dot(adj, margin_ref[...])
    left, right = pack(margin[:, :FREQ], margin[:, FREQ:])
    route("col2", left.astype(jnp.bfloat16), right.astype(jnp.bfloat16), to_a_ref, to_b_ref)
    out_ref[...] = adj


def widen_kernel(adj_ref, fwd_ref, out_ref):
    wide = dot(adj_ref[...], fwd_ref[...])
    out_ref[:FREQ] = wide[:, :TILE]
    out_ref[FREQ:] = wide[:, TILE:]


def fold_kernel(wide_ref, from_a_ref, from_b_ref, patch_ref, out_ref, to_a_ref, to_b_ref):
    from_left, from_right = arrived("col2", from_a_ref, from_b_ref)
    from_left, from_right = from_left.astype(jnp.float32), from_right.astype(jnp.float32)
    low, zero = low_lanes(FREQ), jnp.zeros((FREQ, 128), jnp.float32)
    turned_left, turned_right = pltpu.roll(from_left, 64, 1), pltpu.roll(from_right, 64, 1)
    first_half, second_half = slice(0, FREQ), slice(FREQ, 2 * FREQ)
    for half, left, right in (
        (first_half, turned_left, turned_right),
        (second_half, from_left, from_right),
    ):
        added = wide_ref[half, :128] + jnp.where(low, left, zero)
        out_ref[half, :128] = added.astype(jnp.bfloat16)
        added = wide_ref[half, 128:] + jnp.where(low, zero, right)
        out_ref[half, 128:] = added.astype(jnp.bfloat16)
    wide = out_ref[...]
    top = dot(patch_ref[:MARGIN], wide).astype(jnp.bfloat16)
    bottom = dot(patch_ref[MARGIN + TILE :], wide).astype(jnp.bfloat16)
    route("row2", top, bottom, to_a_ref, to_b_ref)


def core_kernel(wide_ref, patch_ref, mask_ref, out_ref, rim_ref, rate_ref, rows_ref, sem):
    wide = wide_ref[...]
    ends = (slice(0, MARGIN), slice(MARGIN, TILE - MARGIN), slice(TILE - MARGIN, TILE))
    for i, rows in enumerate(ends):
        shifted = slice(rows.start + MARGIN, rows.stop + MARGIN)
        mask = mask_ref[rows]
        squashed = jax.nn.sigmoid(STEEPNESS * mask)
        rate = STEP_RATE * (2.0 * STEEPNESS) * squashed * (1.0 - squashed)
        updated = mask - dot(patch_ref[shifted], wide) * rate
        if i == 1:
            rows_ref[...] = updated
        else:
            rim_ref[i // 2], rate_ref[i // 2] = updated, rate
    copy = pltpu.make_async_copy(rows_ref, out_ref.at[pl.ds(MARGIN, TILE - 2 * MARGIN)], sem)
    copy.start()
    copy.wait()


def finish_kernel(most_ref, rim_ref, rate_ref, from_a_ref, from_b_ref, out_ref, rows_ref, sems):
    del most_ref
    copies = []
    for i, strip in enumerate(arrived("row2", from_a_ref, from_b_ref)):
        rows_ref[i] = rim_ref[i] - strip.astype(jnp.float32) * rate_ref[i]
        start = i * (TILE - MARGIN)
        copy = pltpu.make_async_copy(rows_ref.at[i], out_ref.at[pl.ds(start, MARGIN)], sems.at[i])
        copy.start()
        copies.append(copy)
    for copy in copies:
        copy.wait()


def pairings(mesh):
    wins, rows, cols = (mesh.shape[axis] for axis in AXES)

    def flat(win, row, col):
        return (win * rows + row) * cols + col

    def row_partner(win, row, col, ahead):
        other = row + 1 if ahead else row - 1
        return flat(win, other, col) if 0 <= other < rows else flat(win, row, col ^ 1)

    def col_partner(win, row, col, ahead):
        return flat(win, row, (col + 1 if ahead else col - 1) % cols)

    pairs = {}
    for phase, turned in TURNED.items():
        for swap in range(2):
            pairs[phase, swap] = []
            for place in itertools.product(range(wins), range(rows), range(cols)):
                win, row, col = place
                along = row if phase[:3] == "row" else col
                ahead = (along + turned[win % 2] + swap) % 2 == 0
                partner = row_partner if phase[:3] == "row" else col_partner
                pairs[phase, swap].append((flat(*place), partner(*place, ahead)))
    return pairs


def solution(mesh):
    assert mesh.shape["row"] % 2 == 0 and mesh.shape["col"] % 2 == 0
    pairs = pairings(mesh)
    tables = table_constants()
    bf16, f32 = jnp.bfloat16, jnp.float32
    shape = jax.ShapeDtypeStruct
    edge, strip = shape((MARGIN, TILE), bf16), shape((FREQ, 128), bf16)
    whole = shape((TILE, TILE), f32)
    dma = pltpu.SemaphoreType.DMA

    def swap(phase, to_a, to_b):
        return (
            lax.ppermute(to_a, AXES, pairs[phase, 0]),
            lax.ppermute(to_b, AXES, pairs[phase, 1]),
        )

    def local(mask_params, layout, kernels):
        edges = call(
            edges_kernel, (edge, edge), (mask_params,), 2 * MIB, "edges", hbm=(0,),
            scratch=(pltpu.VMEM((2, MARGIN, TILE), f32), dma((2,))),
        )
        kern = jnp.transpose(kernels, (0, 2, 1, 3))
        part = shape(kern.shape[1:], f32)

        def like(*arrays):
            return tuple(shape(array.shape, array.dtype) for array in arrays)

        inner, rim, patch, fwd, bwd, margin, image = (jnp.asarray(table) for table in tables.values())
        level, rows, inner, rim, patch, fwd, kern_re = call(
            prepare_kernel,
            (whole, whole, *like(inner, rim, patch, fwd), part),
            (mask_params, layout[0, 0], inner, rim, patch, fwd, kern),
            8 * MIB,
            "prepare",
            hbm=range(7),
            scratch=(
                pltpu.VMEM((TILE, TILE), f32),
                pltpu.VMEM(layout.shape[2:], jnp.int32),
                dma((7,)),
            ),
            flops=1_000_000_000,
            moved=1_500_000,
        )
        rows, *strips = call(
            strips_kernel,
            (shape((2 * FREQ, TILE), bf16), strip, strip),
            (rows, *swap("row1", *edges), rim),
            2 * MIB,
            "strips",
        )
        inside, bwd, margin, image, kern_im = call(
            inside_kernel,
            (whole, *like(bwd, margin, image), part),
            (rows, patch, bwd, margin, image, kern),
            8 * MIB,
            "inside",
            hbm=range(2, 6),
            scratch=(dma((4,)),),
            flops=1_000_000_000,
            moved=1_500_000,
        )
        *strips, adj = call(
            tile_kernel,
            (strip, strip, shape((FREQ, 2 * FREQ), bf16)),
            (
                inside,
                *swap("col1", *strips),
                level,
                kern_re,
                kern_im,
                inner,
                patch,
                fwd,
                bwd,
                margin,
                image,
            ),
            32 * MIB,
            "tile",
            scratch=(
                pltpu.VMEM((KERNELS, 2 * TILE, TILE), f32),
                pltpu.VMEM((TILE, TILE), f32),
                pltpu.VMEM((TILE, TILE), f32),
                pltpu.VMEM((2, FREQ, FREQ), f32),
                pltpu.VMEM((2, FREQ, FREQ), f32),
                *[pltpu.VMEM((2 * FREQ, 2 * FREQ), bf16)] * 2,
                *[pltpu.VMEM((2, 2 * FREQ, TILE), bf16)] * 2,
                *[pltpu.VMEM((2 * TILE, 2 * TILE), bf16)] * 2,
                *[pltpu.VMEM((2 * TILE, 2 * FREQ), bf16)] * 2,
            ),
            flops=2_500_000_000,
            moved=8_000_000,
        )
        (wide,) = call(
            widen_kernel, (whole,), (adj, fwd), 2 * MIB, "widen",
            flops=100_000_000, moved=600_000,
        )
        wide, *edges = call(
            fold_kernel,
            (shape((2 * FREQ, TILE), bf16), edge, edge),
            (wide, *swap("col2", *strips), patch),
            4 * MIB,
            "fold",
        )
        ends = shape((2, MARGIN, TILE), f32)
        most, rim, rate = call(
            core_kernel,
            (whole, ends, ends),
            (wide, patch, mask_params),
            4 * MIB,
            "core",
            hbm_out=(0,),
            scratch=(pltpu.VMEM((TILE - 2 * MARGIN, TILE), f32), dma(())),
            flops=200_000_000,
            moved=1_000_000,
        )
        (updated,) = call(
            finish_kernel,
            (whole,),
            (most, rim, rate, *swap("row2", *edges)),
            4 * MIB,
            "finish",
            hbm=(0,),
            hbm_out=(0,),
            scratch=(pltpu.VMEM((2, MARGIN, TILE), f32), dma((2,))),
            input_output_aliases={0: 0},
        )
        return updated

    in_specs = (P(("win", "row"), "col"), P(("win", "row"), "col", None, None), P())
    out_specs = P(("win", "row"), "col")
    return jax.shard_map(local, mesh=mesh, in_specs=in_specs, out_specs=out_specs, check_vma=False)
```

```python
import itertools
import math

import jax
import jax.numpy as jnp
import ml_dtypes
import numpy as np
from jax import lax
from jax.experimental import pallas as pl
from jax.experimental.pallas import tpu as pltpu
from jax.sharding import PartitionSpec as P

TILE = 256
MARGIN = 64
PERIOD = 384
FREQ = 128
KERNELS = 12
STEEPNESS = 2.0
CONTRAST = 4.0
THRESHOLD = 0.75
STEP_RATE = 1.0

AXES = ("win", "row", "col")
MIB = 1 << 20
BLOCK = 64
TURNED = {"row1": (0, 0), "col1": (0, 0), "col2": (1, 1), "row2": (0, 0)}


def table_constants():
    frequency = np.arange(FREQ, dtype=np.int64) - FREQ // 2
    places = np.arange(PERIOD, dtype=np.int64)
    angles = np.mod(frequency[:, None] * places[None, :], PERIOD) * (2.0 * math.pi / PERIOD)
    cos_t = np.cos(angles).astype(np.float32)
    sin_t = np.sin(angles).astype(np.float32)
    inner = np.arange(MARGIN, MARGIN + TILE)
    rim = np.concatenate([np.arange(MARGIN), np.arange(MARGIN + TILE, PERIOD)])
    ci, si, cm, sm = cos_t[:, inner], sin_t[:, inner], cos_t[:, rim], sin_t[:, rim]
    names = dict(
        inner=np.concatenate([ci, si], axis=0),
        rim=np.concatenate([cm, sm], axis=0),
        patch=np.concatenate([cos_t.T, -sin_t.T], axis=1),
        fwd=np.block([[ci, si], [-si, ci]]),
        bwd=np.block([[ci.T, -si.T], [si.T, ci.T]]),
        margin=np.block([[cm, sm], [-sm, cm]]),
    )
    names["image"] = names["bwd"].reshape(2, TILE // BLOCK, BLOCK, -1).swapaxes(0, 1).reshape(2 * TILE, -1)
    return {name: value.astype(ml_dtypes.bfloat16) for name, value in names.items()}


def dot(left, right):
    return jnp.dot(left, right, preferred_element_type=jnp.float32)


VMEM = pl.BlockSpec(memory_space=pltpu.VMEM)
HBM = pl.BlockSpec(memory_space=pltpu.HBM)


def call(kernel, outs, args, limit, name, scratch=(), flops=0, moved=0, hbm=(), hbm_out=(), flags=None, **more):
    args = [
        pltpu.with_memory_space_constraint(arg, pltpu.HBM) if i in hbm else arg
        for i, arg in enumerate(args)
    ]
    return pl.pallas_call(
        kernel,
        out_shape=outs,
        in_specs=[HBM if i in hbm else VMEM for i in range(len(args))],
        out_specs=tuple(HBM if i in hbm_out else VMEM for i in range(len(outs))),
        scratch_shapes=list(scratch),
        compiler_params=pltpu.CompilerParams(vmem_limit_bytes=limit, flags=flags),
        cost_estimate=pl.CostEstimate(flops=flops, bytes_accessed=moved, transcendentals=0),
        name=name,
        **more,
    )(*args)


def first_is_ahead(phase):
    turned = jnp.where(lax.rem(lax.axis_index("win"), 2) == 0, *TURNED[phase])
    return lax.rem(lax.axis_index(phase[:3]) + turned, 2) == 0


def route(phase, back, ahead, to_a_ref, to_b_ref):
    ahead_first = first_is_ahead(phase)
    to_a_ref[...] = jnp.where(ahead_first, ahead, back)
    to_b_ref[...] = jnp.where(ahead_first, back, ahead)


def arrived(phase, from_a_ref, from_b_ref):
    axis = phase[:3]
    ahead_first, at, size = first_is_ahead(phase), lax.axis_index(axis), lax.axis_size(axis)
    a, b = from_a_ref[...], from_b_ref[...]
    zero = jnp.zeros_like(a)
    before = jnp.where(at == 0, zero, jnp.where(ahead_first, b, a))
    after = jnp.where(at == size - 1, zero, jnp.where(ahead_first, a, b))
    return before, after


def low_lanes(rows):
    return lax.broadcasted_iota(jnp.int32, (rows, 128), 1) < 64


def pack(first, second):
    low, turned = low_lanes(FREQ), pltpu.roll(second, 64, 1)
    return jnp.where(low, first, turned), jnp.where(low, turned, first)


def to_transmit(mask):
    return jnp.tanh((STEEPNESS / 2.0) * mask).astype(jnp.bfloat16)


def edges_kernel(mask_ref, to_a_ref, to_b_ref, rows_ref, sems):
    starts = (0, TILE - MARGIN)
    copies = fetch(
        [(mask_ref.at[pl.ds(start, MARGIN)], rows_ref.at[i]) for i, start in enumerate(starts)],
        sems,
    )
    for copy in copies:
        copy.wait()
    route("row1", to_transmit(rows_ref[0]), to_transmit(rows_ref[1]), to_a_ref, to_b_ref)


def fetch(moves, sems):
    copies = [
        pltpu.make_async_copy(source, dest, sems.at[i]) for i, (source, dest) in enumerate(moves)
    ]
    for copy in copies:
        copy.start()
    return copies


def prepare_kernel(
    mask_ref, rect_ref, inner_ref, rim_ref, patch_ref, fwd_ref, kern_ref,
    level_ref, rows_ref, to_inner_ref, to_rim_ref, to_patch_ref, to_fwd_ref, to_kern_ref,
    mask_buf, rect_buf, sems,
):
    rects_in, mask_in, inner_in, *others = fetch(
        (
            (rect_ref, rect_buf),
            (mask_ref, mask_buf),
            (inner_ref, to_inner_ref),
            (rim_ref, to_rim_ref),
            (patch_ref, to_patch_ref),
            (fwd_ref, to_fwd_ref),
            (kern_ref.at[0], to_kern_ref),
        ),
        sems,
    )
    rects_in.wait()
    rects = rect_buf[...]
    places = lax.broadcasted_iota(jnp.int32, (TILE, rects.shape[1]), 0)
    row_in = ((places >= rects[0:1]) & (places < rects[1:2])).astype(jnp.bfloat16)
    col_in = ((places >= rects[2:3]) & (places < rects[3:4])).astype(jnp.bfloat16)
    covered = lax.dot_general(
        row_in, col_in, (((1,), (1,)), ((), ())), preferred_element_type=jnp.float32
    )
    level_ref[...] = 1.0 - 2.0 * jnp.minimum(covered, 1.0)
    mask_in.wait()
    transmit = to_transmit(mask_buf[...])
    inner_in.wait()
    rows_ref[...] = dot(to_inner_ref[...], transmit)
    for copy in others:
        copy.wait()


def strips_kernel(rows_ref, from_a_ref, from_b_ref, rim_ref, out_ref, to_a_ref, to_b_ref):
    above, below = arrived("row1", from_a_ref, from_b_ref)
    halo = jnp.concatenate([above, below], axis=0)
    parts = []
    for half in (slice(0, FREQ), slice(FREQ, 2 * FREQ)):
        part = (rows_ref[half] + dot(rim_ref[half], halo)).astype(jnp.bfloat16)
        out_ref[half] = part
        parts.append(part)
    low = low_lanes(FREQ)
    first, second = (jnp.where(low, part[:, :128], part[:, 128:]) for part in parts)
    left, right = pack(first, second)
    route("col1", left, right, to_a_ref, to_b_ref)


def inside_kernel(
    rows_ref, patch_ref, bwd_ref, margin_ref, image_ref, kern_ref,
    out_ref, to_bwd_ref, to_margin_ref, to_image_ref, to_kern_ref, sems,
):
    copies = fetch(
        (
            (bwd_ref, to_bwd_ref),
            (margin_ref, to_margin_ref),
            (image_ref, to_image_ref),
            (kern_ref.at[1], to_kern_ref),
        ),
        sems,
    )
    for half in (slice(0, FREQ), slice(FREQ, 2 * FREQ)):
        out_ref[half] = dot(rows_ref[half], patch_ref[MARGIN : MARGIN + TILE])
    for copy in copies:
        copy.wait()


def pipeline(groups, first, second, third):
    def step(at, parity):
        static = isinstance(at, int)
        if not static or -1 <= at < groups - 1:
            second(at + 1, 1 - parity)
        if not static or at >= 0:
            third(at, parity)
        if not static or at < groups - 2:
            first(at + 2, parity)

    for at in range(-2, groups):
        step(at, at % 2)


def tile_kernel(
    inside_ref, from_a_ref, from_b_ref, level_ref, kern_re_ref, kern_im_ref,
    inner_ref, patch_ref, fwd_ref, bwd_ref, margin_ref, image_ref,
    to_a_ref, to_b_ref, out_ref,
    field_ref, bright_ref, weight_ref, spec_ref, adj_ref, *slot_refs,
):
    mixed_refs, line_refs, back_refs, wave_refs = (slot_refs[i : i + 2] for i in (0, 2, 4, 6))
    from_left, from_right = arrived("col1", from_a_ref, from_b_ref)
    low = low_lanes(FREQ)
    head, tail = patch_ref[:MARGIN], patch_ref[MARGIN + TILE :]
    first = dot(jnp.where(low, from_right, from_left), jnp.concatenate([tail, head], axis=0))
    second = dot(jnp.where(low, from_left, from_right), jnp.concatenate([head, tail], axis=0))
    first, second = first + inside_ref[:FREQ], second + inside_ref[FREQ:]
    spec_re = (first[:, :FREQ] + second[:, FREQ:]) / PERIOD
    spec_im = (first[:, FREQ:] - second[:, :FREQ]) / PERIOD
    spec_ref[0], spec_ref[1] = spec_re, spec_im
    groups = KERNELS // 2

    def mix(group, slot):
        for j in range(2):
            k = 2 * group + j
            kern_re, kern_im = kern_re_ref[k], kern_im_ref[k]
            spec_re, spec_im = spec_ref[0], spec_ref[1]
            rows = slice(j * FREQ, (j + 1) * FREQ)
            mixed_re = kern_re * spec_re - kern_im * spec_im
            mixed_im = kern_re * spec_im + kern_im * spec_re
            mixed_refs[slot][rows, :FREQ] = mixed_re.astype(jnp.bfloat16)
            mixed_refs[slot][rows, FREQ:] = mixed_im.astype(jnp.bfloat16)

    def expand(group, slot):
        line = dot(mixed_refs[slot][...], fwd_ref[...]).astype(jnp.bfloat16)
        for j in range(2):
            rows = slice(j * FREQ, (j + 1) * FREQ)
            line_refs[slot][j, :FREQ] = line[rows, :TILE]
            line_refs[slot][j, FREQ:] = line[rows, TILE:]

    def image(group, slot):
        fields = [dot(image_ref[...], line_refs[slot][j]) for j in range(2)]
        for at in range(0, TILE, BLOCK):
            rows = slice(at, at + BLOCK)
            total = bright_ref[rows]
            for j, field in enumerate(fields):
                field_re = field[2 * at : 2 * at + BLOCK]
                field_im = field[2 * at + BLOCK : 2 * at + 2 * BLOCK]
                field_ref[2 * group + j, rows] = field_re
                field_ref[2 * group + j, TILE + at : TILE + at + BLOCK] = field_im
                total = total + (field_re * field_re + field_im * field_im)
            bright_ref[rows] = total

    bright_ref[...] = jnp.zeros_like(bright_ref)
    pipeline(groups, mix, expand, image)

    turn = jnp.tanh(bright_ref[...] * (CONTRAST / (2.0 * KERNELS)) - CONTRAST * THRESHOLD / 2.0)
    weight_ref[...] = (turn + level_ref[...]) * (1.0 - turn * turn)

    def weigh(group, slot):
        for j in range(2):
            rows = slice(j * TILE, (j + 1) * TILE)
            weight = weight_ref[...]
            back_re = field_ref[2 * group + j, :TILE] * weight
            back_im = field_ref[2 * group + j, TILE:] * weight
            back_refs[slot][rows, :TILE] = back_re.astype(jnp.bfloat16)
            back_refs[slot][rows, TILE:] = back_im.astype(jnp.bfloat16)

    def contract(group, slot):
        for j in range(2):
            rows = slice(j * TILE, (j + 1) * TILE)
            wave = dot(back_refs[slot][rows], bwd_ref[...])
            wave_refs[slot][rows] = wave.astype(jnp.bfloat16)

    def respond(group, slot):
        adj_re, adj_im = adj_ref[0], adj_ref[1]
        for j in range(2):
            resp = dot(inner_ref[...], wave_refs[slot][j * TILE : (j + 1) * TILE])
            resp_re = resp[:FREQ, :FREQ] + resp[FREQ:, FREQ:]
            resp_im = resp[:FREQ, FREQ:] - resp[FREQ:, :FREQ]
            kern_re, kern_im = kern_re_ref[2 * group + j], kern_im_ref[2 * group + j]
            adj_re = adj_re + (kern_re * resp_re + kern_im * resp_im)
            adj_im = adj_im + (kern_re * resp_im - kern_im * resp_re)
        adj_ref[0], adj_ref[1] = adj_re, adj_im

    adj_ref[...] = jnp.zeros_like(adj_ref)
    pipeline(groups, weigh, contract, respond)

    scale = (CONTRAST / 4.0) * (2.0 / KERNELS) / PERIOD
    adj = (jnp.concatenate([adj_ref[0], adj_ref[1]], axis=1) * scale).astype(jnp.bfloat16)
    margin = dot(adj, margin_ref[...])
    left, right = pack(margin[:, :FREQ], margin[:, FREQ:])
    route("col2", left.astype(jnp.bfloat16), right.astype(jnp.bfloat16), to_a_ref, to_b_ref)
    out_ref[...] = adj


def widen_kernel(adj_ref, fwd_ref, out_ref):
    wide = dot(adj_ref[...], fwd_ref[...])
    out_ref[:FREQ] = wide[:, :TILE]
    out_ref[FREQ:] = wide[:, TILE:]


def fold_kernel(wide_ref, from_a_ref, from_b_ref, patch_ref, out_ref, to_a_ref, to_b_ref):
    from_left, from_right = arrived("col2", from_a_ref, from_b_ref)
    from_left, from_right = from_left.astype(jnp.float32), from_right.astype(jnp.float32)
    low, zero = low_lanes(FREQ), jnp.zeros((FREQ, 128), jnp.float32)
    turned_left, turned_right = pltpu.roll(from_left, 64, 1), pltpu.roll(from_right, 64, 1)
    first_half, second_half = slice(0, FREQ), slice(FREQ, 2 * FREQ)
    for half, left, right in (
        (first_half, turned_left, turned_right),
        (second_half, from_left, from_right),
    ):
        added = wide_ref[half, :128] + jnp.where(low, left, zero)
        out_ref[half, :128] = added.astype(jnp.bfloat16)
        added = wide_ref[half, 128:] + jnp.where(low, zero, right)
        out_ref[half, 128:] = added.astype(jnp.bfloat16)
    wide = out_ref[...]
    top = dot(patch_ref[:MARGIN], wide).astype(jnp.bfloat16)
    bottom = dot(patch_ref[MARGIN + TILE :], wide).astype(jnp.bfloat16)
    route("row2", top, bottom, to_a_ref, to_b_ref)


def core_kernel(wide_ref, patch_ref, mask_ref, out_ref, rim_ref, rate_ref, rows_ref, sem):
    wide = wide_ref[...]
    ends = (slice(0, MARGIN), slice(MARGIN, TILE - MARGIN), slice(TILE - MARGIN, TILE))
    for i, rows in enumerate(ends):
        shifted = slice(rows.start + MARGIN, rows.stop + MARGIN)
        mask = mask_ref[rows]
        squashed = jax.nn.sigmoid(STEEPNESS * mask)
        rate = STEP_RATE * (2.0 * STEEPNESS) * squashed * (1.0 - squashed)
        updated = mask - dot(patch_ref[shifted], wide) * rate
        if i == 1:
            rows_ref[...] = updated
        else:
            rim_ref[i // 2], rate_ref[i // 2] = updated, rate
    copy = pltpu.make_async_copy(rows_ref, out_ref.at[pl.ds(MARGIN, TILE - 2 * MARGIN)], sem)
    copy.start()
    copy.wait()


def finish_kernel(most_ref, rim_ref, rate_ref, from_a_ref, from_b_ref, out_ref, rows_ref, sems):
    del most_ref
    copies = []
    for i, strip in enumerate(arrived("row2", from_a_ref, from_b_ref)):
        rows_ref[i] = rim_ref[i] - strip.astype(jnp.float32) * rate_ref[i]
        start = i * (TILE - MARGIN)
        copy = pltpu.make_async_copy(rows_ref.at[i], out_ref.at[pl.ds(start, MARGIN)], sems.at[i])
        copy.start()
        copies.append(copy)
    for copy in copies:
        copy.wait()


def pairings(mesh):
    wins, rows, cols = (mesh.shape[axis] for axis in AXES)

    def flat(win, row, col):
        return (win * rows + row) * cols + col

    def row_partner(win, row, col, ahead):
        other = row + 1 if ahead else row - 1
        return flat(win, other, col) if 0 <= other < rows else flat(win, row, col ^ 1)

    def col_partner(win, row, col, ahead):
        return flat(win, row, (col + 1 if ahead else col - 1) % cols)

    pairs = {}
    for phase, turned in TURNED.items():
        for swap in range(2):
            pairs[phase, swap] = []
            for place in itertools.product(range(wins), range(rows), range(cols)):
                win, row, col = place
                along = row if phase[:3] == "row" else col
                ahead = (along + turned[win % 2] + swap) % 2 == 0
                partner = row_partner if phase[:3] == "row" else col_partner
                pairs[phase, swap].append((flat(*place), partner(*place, ahead)))
    return pairs


def solution(mesh):
    assert mesh.shape["row"] % 2 == 0 and mesh.shape["col"] % 2 == 0
    pairs = pairings(mesh)
    tables = table_constants()
    bf16, f32 = jnp.bfloat16, jnp.float32
    shape = jax.ShapeDtypeStruct
    edge, strip = shape((MARGIN, TILE), bf16), shape((FREQ, 128), bf16)
    whole = shape((TILE, TILE), f32)
    dma = pltpu.SemaphoreType.DMA

    def swap(phase, to_a, to_b):
        return (
            lax.ppermute(to_a, AXES, pairs[phase, 0]),
            lax.ppermute(to_b, AXES, pairs[phase, 1]),
        )

    def local(mask_params, layout, kernels):
        edges = call(
            edges_kernel, (edge, edge), (mask_params,), 2 * MIB, "edges", hbm=(0,),
            scratch=(pltpu.VMEM((2, MARGIN, TILE), f32), dma((2,))),
        )
        kern = jnp.transpose(kernels, (0, 2, 1, 3))
        part = shape(kern.shape[1:], f32)

        def like(*arrays):
            return tuple(shape(array.shape, array.dtype) for array in arrays)

        inner, rim, patch, fwd, bwd, margin, image = (jnp.asarray(table) for table in tables.values())
        level, rows, inner, rim, patch, fwd, kern_re = call(
            prepare_kernel,
            (whole, whole, *like(inner, rim, patch, fwd), part),
            (mask_params, layout[0, 0], inner, rim, patch, fwd, kern),
            8 * MIB,
            "prepare",
            hbm=range(7),
            scratch=(
                pltpu.VMEM((TILE, TILE), f32),
                pltpu.VMEM(layout.shape[2:], jnp.int32),
                dma((7,)),
            ),
            flops=1_000_000_000,
            moved=1_500_000,
        )
        rows, *strips = call(
            strips_kernel,
            (shape((2 * FREQ, TILE), bf16), strip, strip),
            (rows, *swap("row1", *edges), rim),
            2 * MIB,
            "strips",
        )
        inside, bwd, margin, image, kern_im = call(
            inside_kernel,
            (whole, *like(bwd, margin, image), part),
            (rows, patch, bwd, margin, image, kern),
            8 * MIB,
            "inside",
            hbm=range(2, 6),
            scratch=(dma((4,)),),
            flops=1_000_000_000,
            moved=1_500_000,
        )
        *strips, adj = call(
            tile_kernel,
            (strip, strip, shape((FREQ, 2 * FREQ), bf16)),
            (
                inside,
                *swap("col1", *strips),
                level,
                kern_re,
                kern_im,
                inner,
                patch,
                fwd,
                bwd,
                margin,
                image,
            ),
            32 * MIB,
            "tile",
            scratch=(
                pltpu.VMEM((KERNELS, 2 * TILE, TILE), f32),
                pltpu.VMEM((TILE, TILE), f32),
                pltpu.VMEM((TILE, TILE), f32),
                pltpu.VMEM((2, FREQ, FREQ), f32),
                pltpu.VMEM((2, FREQ, FREQ), f32),
                *[pltpu.VMEM((2 * FREQ, 2 * FREQ), bf16)] * 2,
                *[pltpu.VMEM((2, 2 * FREQ, TILE), bf16)] * 2,
                *[pltpu.VMEM((2 * TILE, 2 * TILE), bf16)] * 2,
                *[pltpu.VMEM((2 * TILE, 2 * FREQ), bf16)] * 2,
            ),
            flops=2_500_000_000,
            moved=8_000_000,
        )
        (wide,) = call(
            widen_kernel, (whole,), (adj, fwd), 2 * MIB, "widen",
            flops=100_000_000, moved=600_000,
        )
        wide, *edges = call(
            fold_kernel,
            (shape((2 * FREQ, TILE), bf16), edge, edge),
            (wide, *swap("col2", *strips), patch),
            4 * MIB,
            "fold",
        )
        ends = shape((2, MARGIN, TILE), f32)
        most, rim, rate = call(
            core_kernel,
            (whole, ends, ends),
            (wide, patch, mask_params),
            4 * MIB,
            "core",
            hbm_out=(0,),
            scratch=(pltpu.VMEM((TILE - 2 * MARGIN, TILE), f32), dma(())),
            flops=200_000_000,
            moved=1_000_000,
        )
        (updated,) = call(
            finish_kernel,
            (whole,),
            (most, rim, rate, *swap("row2", *edges)),
            4 * MIB,
            "finish",
            hbm=(0,),
            hbm_out=(0,),
            scratch=(pltpu.VMEM((2, MARGIN, TILE), f32), dma((2,))),
            input_output_aliases={0: 0},
        )
        return updated

    in_specs = (P(("win", "row"), "col"), P(("win", "row"), "col", None, None), P())
    out_specs = P(("win", "row"), "col")
    return jax.shard_map(local, mesh=mesh, in_specs=in_specs, out_specs=out_specs, check_vma=False)
```

```python
import itertools
import math

import jax
import jax.numpy as jnp
import ml_dtypes
import numpy as np
from jax import lax
from jax.experimental import pallas as pl
from jax.experimental.pallas import tpu as pltpu
from jax.sharding import PartitionSpec as P

TILE = 256
MARGIN = 64
PERIOD = 384
FREQ = 128
KERNELS = 12
STEEPNESS = 2.0
CONTRAST = 4.0
THRESHOLD = 0.75
STEP_RATE = 1.0

AXES = ("win", "row", "col")
MIB = 1 << 20
BLOCK = 64
TURNED = {"row1": (0, 0), "col1": (0, 0), "col2": (1, 1), "row2": (0, 0)}


def table_constants():
    frequency = np.arange(FREQ, dtype=np.int64) - FREQ // 2
    places = np.arange(PERIOD, dtype=np.int64)
    angles = np.mod(frequency[:, None] * places[None, :], PERIOD) * (2.0 * math.pi / PERIOD)
    cos_t = np.cos(angles).astype(np.float32)
    sin_t = np.sin(angles).astype(np.float32)
    inner = np.arange(MARGIN, MARGIN + TILE)
    rim = np.concatenate([np.arange(MARGIN), np.arange(MARGIN + TILE, PERIOD)])
    ci, si, cm, sm = cos_t[:, inner], sin_t[:, inner], cos_t[:, rim], sin_t[:, rim]
    names = dict(
        inner=np.concatenate([ci, si], axis=0),
        rim=np.concatenate([cm, sm], axis=0),
        patch=np.concatenate([cos_t.T, -sin_t.T], axis=1),
        fwd=np.block([[ci, si], [-si, ci]]),
        bwd=np.block([[ci.T, -si.T], [si.T, ci.T]]),
        margin=np.block([[cm, sm], [-sm, cm]]),
    )
    return {name: value.astype(ml_dtypes.bfloat16) for name, value in names.items()}


def dot(left, right):
    return jnp.dot(left, right, preferred_element_type=jnp.float32)


VMEM = pl.BlockSpec(memory_space=pltpu.VMEM)
HBM = pl.BlockSpec(memory_space=pltpu.HBM)


def call(kernel, outs, args, limit, name, scratch=(), flops=0, moved=0, hbm=(), hbm_out=(), flags=None, **more):
    args = [
        pltpu.with_memory_space_constraint(arg, pltpu.HBM) if i in hbm else arg
        for i, arg in enumerate(args)
    ]
    return pl.pallas_call(
        kernel,
        out_shape=outs,
        in_specs=[HBM if i in hbm else VMEM for i in range(len(args))],
        out_specs=tuple(HBM if i in hbm_out else VMEM for i in range(len(outs))),
        scratch_shapes=list(scratch),
        compiler_params=pltpu.CompilerParams(vmem_limit_bytes=limit, flags=flags),
        cost_estimate=pl.CostEstimate(flops=flops, bytes_accessed=moved, transcendentals=0),
        name=name,
        **more,
    )(*args)


def first_is_ahead(phase):
    turned = jnp.where(lax.rem(lax.axis_index("win"), 2) == 0, *TURNED[phase])
    return lax.rem(lax.axis_index(phase[:3]) + turned, 2) == 0


def route(phase, back, ahead, to_a_ref, to_b_ref):
    ahead_first = first_is_ahead(phase)
    to_a_ref[...] = jnp.where(ahead_first, ahead, back)
    to_b_ref[...] = jnp.where(ahead_first, back, ahead)


def arrived(phase, from_a_ref, from_b_ref):
    axis = phase[:3]
    ahead_first, at, size = first_is_ahead(phase), lax.axis_index(axis), lax.axis_size(axis)
    a, b = from_a_ref[...], from_b_ref[...]
    zero = jnp.zeros_like(a)
    before = jnp.where(at == 0, zero, jnp.where(ahead_first, b, a))
    after = jnp.where(at == size - 1, zero, jnp.where(ahead_first, a, b))
    return before, after


def low_lanes(rows):
    return lax.broadcasted_iota(jnp.int32, (rows, 128), 1) < 64


def pack(first, second):
    low, turned = low_lanes(FREQ), pltpu.roll(second, 64, 1)
    return jnp.where(low, first, turned), jnp.where(low, turned, first)


def to_transmit(mask):
    return jnp.tanh((STEEPNESS / 2.0) * mask).astype(jnp.bfloat16)


def edges_kernel(mask_ref, to_a_ref, to_b_ref, rows_ref, sems):
    starts = (0, TILE - MARGIN)
    copies = fetch(
        [(mask_ref.at[pl.ds(start, MARGIN)], rows_ref.at[i]) for i, start in enumerate(starts)],
        sems,
    )
    for copy in copies:
        copy.wait()
    route("row1", to_transmit(rows_ref[0]), to_transmit(rows_ref[1]), to_a_ref, to_b_ref)


def fetch(moves, sems):
    copies = [
        pltpu.make_async_copy(source, dest, sems.at[i]) for i, (source, dest) in enumerate(moves)
    ]
    for copy in copies:
        copy.start()
    return copies


def prepare_kernel(
    mask_ref, rect_ref, inner_ref, rim_ref, patch_ref, fwd_ref, kern_ref,
    level_ref, rows_ref, to_inner_ref, to_rim_ref, to_patch_ref, to_fwd_ref, to_kern_ref,
    mask_buf, rect_buf, sems,
):
    rects_in, mask_in, inner_in, *others = fetch(
        (
            (rect_ref, rect_buf),
            (mask_ref, mask_buf),
            (inner_ref, to_inner_ref),
            (rim_ref, to_rim_ref),
            (patch_ref, to_patch_ref),
            (fwd_ref, to_fwd_ref),
            (kern_ref.at[0], to_kern_ref),
        ),
        sems,
    )
    rects_in.wait()
    rects = rect_buf[...]
    places = lax.broadcasted_iota(jnp.int32, (TILE, rects.shape[1]), 0)
    row_in = ((places >= rects[0:1]) & (places < rects[1:2])).astype(jnp.bfloat16)
    col_in = ((places >= rects[2:3]) & (places < rects[3:4])).astype(jnp.bfloat16)
    covered = lax.dot_general(
        row_in, col_in, (((1,), (1,)), ((), ())), preferred_element_type=jnp.float32
    )
    level_ref[...] = 1.0 - 2.0 * jnp.minimum(covered, 1.0)
    mask_in.wait()
    transmit = to_transmit(mask_buf[...])
    inner_in.wait()
    rows_ref[...] = dot(to_inner_ref[...], transmit)
    for copy in others:
        copy.wait()


def strips_kernel(rows_ref, from_a_ref, from_b_ref, rim_ref, out_ref, to_a_ref, to_b_ref):
    above, below = arrived("row1", from_a_ref, from_b_ref)
    halo = jnp.concatenate([above, below], axis=0)
    parts = []
    for half in (slice(0, FREQ), slice(FREQ, 2 * FREQ)):
        part = (rows_ref[half] + dot(rim_ref[half], halo)).astype(jnp.bfloat16)
        out_ref[half] = part
        parts.append(part)
    low = low_lanes(FREQ)
    first, second = (jnp.where(low, part[:, :128], part[:, 128:]) for part in parts)
    left, right = pack(first, second)
    route("col1", left, right, to_a_ref, to_b_ref)


def inside_kernel(
    rows_ref, patch_ref, bwd_ref, margin_ref, kern_ref,
    out_ref, to_bwd_ref, to_margin_ref, to_image_ref, to_kern_ref, sems,
):
    copies = fetch(
        (
            (bwd_ref, to_bwd_ref),
            (margin_ref, to_margin_ref),
            (kern_ref.at[1], to_kern_ref),
        ),
        sems,
    )
    for half in (slice(0, FREQ), slice(FREQ, 2 * FREQ)):
        out_ref[half] = dot(rows_ref[half], patch_ref[MARGIN : MARGIN + TILE])
    copies[0].wait()
    for at in range(0, TILE, BLOCK):
        to_image_ref[2 * at : 2 * at + BLOCK] = to_bwd_ref[at : at + BLOCK]
        to_image_ref[2 * at + BLOCK : 2 * at + 2 * BLOCK] = to_bwd_ref[TILE + at : TILE + at + BLOCK]
    for copy in copies[1:]:
        copy.wait()


def pipeline(groups, first, second, third):
    def step(at, parity):
        static = isinstance(at, int)
        if not static or -1 <= at < groups - 1:
            second(at + 1, 1 - parity)
        if not static or at >= 0:
            third(at, parity)
        if not static or at < groups - 2:
            first(at + 2, parity)

    for at in range(-2, groups):
        step(at, at % 2)


def tile_kernel(
    inside_ref, from_a_ref, from_b_ref, level_ref, kern_re_ref, kern_im_ref,
    inner_ref, patch_ref, fwd_ref, bwd_ref, margin_ref, image_ref,
    to_a_ref, to_b_ref, out_ref,
    field_ref, bright_ref, weight_ref, spec_ref, adj_ref, *slot_refs,
):
    mixed_refs, line_refs, back_refs, wave_refs = (slot_refs[i : i + 2] for i in (0, 2, 4, 6))
    from_left, from_right = arrived("col1", from_a_ref, from_b_ref)
    low = low_lanes(FREQ)
    head, tail = patch_ref[:MARGIN], patch_ref[MARGIN + TILE :]
    first = dot(jnp.where(low, from_right, from_left), jnp.concatenate([tail, head], axis=0))
    second = dot(jnp.where(low, from_left, from_right), jnp.concatenate([head, tail], axis=0))
    first, second = first + inside_ref[:FREQ], second + inside_ref[FREQ:]
    spec_re = (first[:, :FREQ] + second[:, FREQ:]) / PERIOD
    spec_im = (first[:, FREQ:] - second[:, :FREQ]) / PERIOD
    spec_ref[0], spec_ref[1] = spec_re, spec_im
    groups = KERNELS // 2

    def mix(group, slot):
        for j in range(2):
            k = 2 * group + j
            kern_re, kern_im = kern_re_ref[k], kern_im_ref[k]
            spec_re, spec_im = spec_ref[0], spec_ref[1]
            rows = slice(j * FREQ, (j + 1) * FREQ)
            mixed_re = kern_re * spec_re - kern_im * spec_im
            mixed_im = kern_re * spec_im + kern_im * spec_re
            mixed_refs[slot][rows, :FREQ] = mixed_re.astype(jnp.bfloat16)
            mixed_refs[slot][rows, FREQ:] = mixed_im.astype(jnp.bfloat16)

    def expand(group, slot):
        line = dot(mixed_refs[slot][...], fwd_ref[...]).astype(jnp.bfloat16)
        for j in range(2):
            rows = slice(j * FREQ, (j + 1) * FREQ)
            line_refs[slot][j, :FREQ] = line[rows, :TILE]
            line_refs[slot][j, FREQ:] = line[rows, TILE:]

    def image(group, slot):
        fields = [dot(image_ref[...], line_refs[slot][j]) for j in range(2)]
        for at in range(0, TILE, BLOCK):
            rows = slice(at, at + BLOCK)
            total = bright_ref[rows]
            for j, field in enumerate(fields):
                field_re = field[2 * at : 2 * at + BLOCK]
                field_im = field[2 * at + BLOCK : 2 * at + 2 * BLOCK]
                field_ref[2 * group + j, rows] = field_re
                field_ref[2 * group + j, TILE + at : TILE + at + BLOCK] = field_im
                total = total + (field_re * field_re + field_im * field_im)
            bright_ref[rows] = total

    bright_ref[...] = jnp.zeros_like(bright_ref)
    pipeline(groups, mix, expand, image)

    turn = jnp.tanh(bright_ref[...] * (CONTRAST / (2.0 * KERNELS)) - CONTRAST * THRESHOLD / 2.0)
    weight_ref[...] = (turn + level_ref[...]) * (1.0 - turn * turn)

    def weigh(group, slot):
        for j in range(2):
            rows = slice(j * TILE, (j + 1) * TILE)
            weight = weight_ref[...]
            back_re = field_ref[2 * group + j, :TILE] * weight
            back_im = field_ref[2 * group + j, TILE:] * weight
            back_refs[slot][rows, :TILE] = back_re.astype(jnp.bfloat16)
            back_refs[slot][rows, TILE:] = back_im.astype(jnp.bfloat16)

    def contract(group, slot):
        for j in range(2):
            rows = slice(j * TILE, (j + 1) * TILE)
            wave = dot(back_refs[slot][rows], bwd_ref[...])
            wave_refs[slot][rows] = wave.astype(jnp.bfloat16)

    def respond(group, slot):
        adj_re, adj_im = adj_ref[0], adj_ref[1]
        for j in range(2):
            resp = dot(inner_ref[...], wave_refs[slot][j * TILE : (j + 1) * TILE])
            resp_re = resp[:FREQ, :FREQ] + resp[FREQ:, FREQ:]
            resp_im = resp[:FREQ, FREQ:] - resp[FREQ:, :FREQ]
            kern_re, kern_im = kern_re_ref[2 * group + j], kern_im_ref[2 * group + j]
            adj_re = adj_re + (kern_re * resp_re + kern_im * resp_im)
            adj_im = adj_im + (kern_re * resp_im - kern_im * resp_re)
        adj_ref[0], adj_ref[1] = adj_re, adj_im

    adj_ref[...] = jnp.zeros_like(adj_ref)
    pipeline(groups, weigh, contract, respond)

    scale = (CONTRAST / 4.0) * (2.0 / KERNELS) / PERIOD
    adj = (jnp.concatenate([adj_ref[0], adj_ref[1]], axis=1) * scale).astype(jnp.bfloat16)
    margin = dot(adj, margin_ref[...])
    left, right = pack(margin[:, :FREQ], margin[:, FREQ:])
    route("col2", left.astype(jnp.bfloat16), right.astype(jnp.bfloat16), to_a_ref, to_b_ref)
    out_ref[...] = adj


def widen_kernel(adj_ref, fwd_ref, out_ref):
    wide = dot(adj_ref[...], fwd_ref[...])
    out_ref[:FREQ] = wide[:, :TILE]
    out_ref[FREQ:] = wide[:, TILE:]


def fold_kernel(wide_ref, from_a_ref, from_b_ref, patch_ref, out_ref, to_a_ref, to_b_ref):
    from_left, from_right = arrived("col2", from_a_ref, from_b_ref)
    from_left, from_right = from_left.astype(jnp.float32), from_right.astype(jnp.float32)
    low, zero = low_lanes(FREQ), jnp.zeros((FREQ, 128), jnp.float32)
    turned_left, turned_right = pltpu.roll(from_left, 64, 1), pltpu.roll(from_right, 64, 1)
    first_half, second_half = slice(0, FREQ), slice(FREQ, 2 * FREQ)
    for half, left, right in (
        (first_half, turned_left, turned_right),
        (second_half, from_left, from_right),
    ):
        added = wide_ref[half, :128] + jnp.where(low, left, zero)
        out_ref[half, :128] = added.astype(jnp.bfloat16)
        added = wide_ref[half, 128:] + jnp.where(low, zero, right)
        out_ref[half, 128:] = added.astype(jnp.bfloat16)
    wide = out_ref[...]
    top = dot(patch_ref[:MARGIN], wide).astype(jnp.bfloat16)
    bottom = dot(patch_ref[MARGIN + TILE :], wide).astype(jnp.bfloat16)
    route("row2", top, bottom, to_a_ref, to_b_ref)


def core_kernel(wide_ref, patch_ref, mask_ref, out_ref, rim_ref, rate_ref, rows_ref, sem):
    wide = wide_ref[...]
    ends = (slice(0, MARGIN), slice(MARGIN, TILE - MARGIN), slice(TILE - MARGIN, TILE))
    for i, rows in enumerate(ends):
        shifted = slice(rows.start + MARGIN, rows.stop + MARGIN)
        mask = mask_ref[rows]
        squashed = jax.nn.sigmoid(STEEPNESS * mask)
        rate = STEP_RATE * (2.0 * STEEPNESS) * squashed * (1.0 - squashed)
        updated = mask - dot(patch_ref[shifted], wide) * rate
        if i == 1:
            rows_ref[...] = updated
        else:
            rim_ref[i // 2], rate_ref[i // 2] = updated, rate
    copy = pltpu.make_async_copy(rows_ref, out_ref.at[pl.ds(MARGIN, TILE - 2 * MARGIN)], sem)
    copy.start()
    copy.wait()


def finish_kernel(most_ref, rim_ref, rate_ref, from_a_ref, from_b_ref, out_ref, rows_ref, sems):
    del most_ref
    copies = []
    for i, strip in enumerate(arrived("row2", from_a_ref, from_b_ref)):
        rows_ref[i] = rim_ref[i] - strip.astype(jnp.float32) * rate_ref[i]
        start = i * (TILE - MARGIN)
        copy = pltpu.make_async_copy(rows_ref.at[i], out_ref.at[pl.ds(start, MARGIN)], sems.at[i])
        copy.start()
        copies.append(copy)
    for copy in copies:
        copy.wait()


def pairings(mesh):
    wins, rows, cols = (mesh.shape[axis] for axis in AXES)

    def flat(win, row, col):
        return (win * rows + row) * cols + col

    def row_partner(win, row, col, ahead):
        other = row + 1 if ahead else row - 1
        return flat(win, other, col) if 0 <= other < rows else flat(win, row, col ^ 1)

    def col_partner(win, row, col, ahead):
        return flat(win, row, (col + 1 if ahead else col - 1) % cols)

    pairs = {}
    for phase, turned in TURNED.items():
        for swap in range(2):
            pairs[phase, swap] = []
            for place in itertools.product(range(wins), range(rows), range(cols)):
                win, row, col = place
                along = row if phase[:3] == "row" else col
                ahead = (along + turned[win % 2] + swap) % 2 == 0
                partner = row_partner if phase[:3] == "row" else col_partner
                pairs[phase, swap].append((flat(*place), partner(*place, ahead)))
    return pairs


def solution(mesh):
    assert mesh.shape["row"] % 2 == 0 and mesh.shape["col"] % 2 == 0
    pairs = pairings(mesh)
    tables = table_constants()
    bf16, f32 = jnp.bfloat16, jnp.float32
    shape = jax.ShapeDtypeStruct
    edge, strip = shape((MARGIN, TILE), bf16), shape((FREQ, 128), bf16)
    whole = shape((TILE, TILE), f32)
    dma = pltpu.SemaphoreType.DMA

    def swap(phase, to_a, to_b):
        return (
            lax.ppermute(to_a, AXES, pairs[phase, 0]),
            lax.ppermute(to_b, AXES, pairs[phase, 1]),
        )

    def local(mask_params, layout, kernels):
        edges = call(
            edges_kernel, (edge, edge), (mask_params,), 2 * MIB, "edges", hbm=(0,),
            scratch=(pltpu.VMEM((2, MARGIN, TILE), f32), dma((2,))),
        )
        kern = jnp.transpose(kernels, (0, 2, 1, 3))
        part = shape(kern.shape[1:], f32)

        def like(*arrays):
            return tuple(shape(array.shape, array.dtype) for array in arrays)

        inner, rim, patch, fwd, bwd, margin = (jnp.asarray(table) for table in tables.values())
        level, rows, inner, rim, patch, fwd, kern_re = call(
            prepare_kernel,
            (whole, whole, *like(inner, rim, patch, fwd), part),
            (mask_params, layout[0, 0], inner, rim, patch, fwd, kern),
            8 * MIB,
            "prepare",
            hbm=range(7),
            scratch=(
                pltpu.VMEM((TILE, TILE), f32),
                pltpu.VMEM(layout.shape[2:], jnp.int32),
                dma((7,)),
            ),
            flops=1_000_000_000,
            moved=1_500_000,
        )
        rows, *strips = call(
            strips_kernel,
            (shape((2 * FREQ, TILE), bf16), strip, strip),
            (rows, *swap("row1", *edges), rim),
            2 * MIB,
            "strips",
        )
        inside, bwd, margin, image, kern_im = call(
            inside_kernel,
            (whole, *like(bwd, margin, bwd), part),
            (rows, patch, bwd, margin, kern),
            8 * MIB,
            "inside",
            hbm=range(2, 5),
            scratch=(dma((3,)),),
            flops=1_000_000_000,
            moved=1_500_000,
        )
        *strips, adj = call(
            tile_kernel,
            (strip, strip, shape((FREQ, 2 * FREQ), bf16)),
            (
                inside,
                *swap("col1", *strips),
                level,
                kern_re,
                kern_im,
                inner,
                patch,
                fwd,
                bwd,
                margin,
                image,
            ),
            32 * MIB,
            "tile",
            scratch=(
                pltpu.VMEM((KERNELS, 2 * TILE, TILE), f32),
                pltpu.VMEM((TILE, TILE), f32),
                pltpu.VMEM((TILE, TILE), f32),
                pltpu.VMEM((2, FREQ, FREQ), f32),
                pltpu.VMEM((2, FREQ, FREQ), f32),
                *[pltpu.VMEM((2 * FREQ, 2 * FREQ), bf16)] * 2,
                *[pltpu.VMEM((2, 2 * FREQ, TILE), bf16)] * 2,
                *[pltpu.VMEM((2 * TILE, 2 * TILE), bf16)] * 2,
                *[pltpu.VMEM((2 * TILE, 2 * FREQ), bf16)] * 2,
            ),
            flops=2_500_000_000,
            moved=8_000_000,
        )
        (wide,) = call(
            widen_kernel, (whole,), (adj, fwd), 2 * MIB, "widen",
            flops=100_000_000, moved=600_000,
        )
        wide, *edges = call(
            fold_kernel,
            (shape((2 * FREQ, TILE), bf16), edge, edge),
            (wide, *swap("col2", *strips), patch),
            4 * MIB,
            "fold",
        )
        ends = shape((2, MARGIN, TILE), f32)
        most, rim, rate = call(
            core_kernel,
            (whole, ends, ends),
            (wide, patch, mask_params),
            4 * MIB,
            "core",
            hbm_out=(0,),
            scratch=(pltpu.VMEM((TILE - 2 * MARGIN, TILE), f32), dma(())),
            flops=200_000_000,
            moved=1_000_000,
        )
        (updated,) = call(
            finish_kernel,
            (whole,),
            (most, rim, rate, *swap("row2", *edges)),
            4 * MIB,
            "finish",
            hbm=(0,),
            hbm_out=(0,),
            scratch=(pltpu.VMEM((2, MARGIN, TILE), f32), dma((2,))),
            input_output_aliases={0: 0},
        )
        return updated

    in_specs = (P(("win", "row"), "col"), P(("win", "row"), "col", None, None), P())
    out_specs = P(("win", "row"), "col")
    return jax.shard_map(local, mesh=mesh, in_specs=in_specs, out_specs=out_specs, check_vma=False)
```
